128 devices in a mesh: samp: 32 (over y, x, core), slab: 4 (over z).
Axes of the slice: x: 4, y: 4, z: 4, core: 2. Of those that a mesh axis runs over, the one named last changes fastest.
Arguments:
- ld_blocks: bfloat16 [4, 64, 768, 768], P('slab', 'samp'), may hold values from -1 to 1, as said below
- marginal: float32 [4, 49152], P('slab', 'samp'), may hold values from -1.8 to 1.8
- normals: float32 [2, 4, 49152], P(None, 'slab', 'samp'), may hold values from -6 to 6
- block_len: int32 [64], P('samp'), may hold values from 1 to 768, 36864 in all
- scale_start: float32 [49152], P('samp'), may hold values from 0.2 to 5
- ancestry_weight: float32 [4], replicated, may hold values from 4 to 64
- dosage: bfloat16 [4096, 49152], P('samp', 'slab'), may hold values from 0 to 2
Outputs:
- effects: float32 [4, 49152], P('slab', 'samp')
- shrink: float32 [49152], P('samp')
- scores: float32 [4096, 4], P('samp', 'slab')
The draws below stay inside these ranges and needn't reach their ends.
Inputs may be any that keep to these rules, and one draw needn't show every extreme that they name: `block_len`: the block lengths sum to 36864; the longest is exactly 768. `ld_blocks`: every block is symmetric with unit diagonal, and it and each of its leading principal submatrices is positive definite.
All inputs are finite; a program needn't handle non-finite values.
Results may differ from the reference program's by a relative error of at most 0.0031.
Values may be sent and summed in bfloat16 or wider, within the bound.
A program may use at most 128 MiB of HBM per device.

```python
import math
import jax
import jax.numpy as jnp
import numpy as np
from jax import lax

K = 4
BMAX = 768
SWEEPS = 2
NB = 64
M = 49152
LIVE = 36864
QUART = 384
SAMPLES = 4096
N_SAMP = 32
N_SLAB = 4


def draw_ld_blocks(key, part):
    noise_key = jax.random.fold_in(key, 11)
    rate_key = jax.random.fold_in(key, 23)
    normals = jax.random.normal(noise_key, (K, NB, BMAX, BMAX), jnp.float32)
    rate_low = 0.8
    rate_high = 0.95
    banded_share = 0.7
    rates = jax.random.uniform(rate_key, (K, NB, 1, 1), jnp.float32, rate_low, rate_high)
    position = jnp.arange(BMAX, dtype=jnp.float32)
    distance = jnp.abs(position[:, None] - position[None, :])
    banded = jnp.exp(distance[None, None, :, :] * jnp.log(rates))
    symmetric = (normals + jnp.swapaxes(normals, 2, 3)) * (0.25 / math.sqrt(2.0 * BMAX))
    identity = jnp.eye(BMAX, dtype=jnp.float32)
    scattered = symmetric * (1.0 - identity) + identity
    return (banded_share * banded + (1.0 - banded_share) * scattered).astype(jnp.bfloat16)


def shard_levels(rng, shape, split, smallest, high):
    loudness = 1.0
    for dim, shards_of in split:
        steps = jax.random.uniform(jax.random.fold_in(jax.random.fold_in(rng, 6), dim), (shards_of,), jnp.float32, smallest / len(split), high / len(split))
        loudness = loudness * jnp.repeat(jnp.exp(steps), shape[dim] // shards_of).reshape((-1,) + (1,) * (len(shape) - 1 - dim))
    return loudness


def length_profile(number_of, total, reach, skew):
    portions = [(1 << 20) // math.isqrt(standing ** skew) + 1 for standing in range(2, number_of + 1)]
    spare, holding = total - reach - (number_of - 1), [1] * (number_of - 1)
    while spare > 0:
        free = [i for i in range(number_of - 1) if holding[i] < reach]
        mass, left = sum([portions[i] for i in free]), spare
        for i in free:
            more = min(reach - holding[i], max(1, left * portions[i] // mass), spare)
            holding[i] = holding[i] + more
            spare = spare - more
    return np.array([reach] + holding)


def uneven_parts(own_key, amount, total, reach, lean):
    if amount == 2:
        one = jax.random.randint(own_key, (), max(1, total - reach), min(reach, total - 1) + 1)
        return jnp.stack([one, total - one])
    tallies = jnp.asarray(length_profile(amount, total, reach, lean), jnp.int32)
    pairs = (amount - 1) // 2
    source_of, receiver = tallies[1:1 + 2 * pairs:2], tallies[2:2 + 2 * pairs:2]
    margin = jnp.minimum(source_of - 1, reach - receiver)
    passed = jax.random.randint(jax.random.fold_in(own_key, 1), (pairs,), 0, 1 << 20) % (margin + 1)
    tallies = tallies.at[1:1 + 2 * pairs:2].set(source_of - passed).at[2:2 + 2 * pairs:2].set(receiver + passed)
    return tallies[jax.random.permutation(jax.random.fold_in(own_key, 2), amount)]


def gaussian(rng, shape, scale, reach, split=(), held_as=jnp.bfloat16):
    values = scale * jax.random.normal(rng, shape, jnp.float32)
    if split:
        values = values * shard_levels(rng, shape, split, -0.22, 0.18)
    return jnp.clip(values, -reach, reach).astype(held_as)


def setup_inputs(seed: int = 0) -> dict:
    key_of = jax.random.split(jax.random.key(seed), 8)
    return {
        "ld_blocks": draw_ld_blocks(jax.random.fold_in(key_of[7], 71), 0),
        "marginal": gaussian(key_of[1], (K, M), 0.3, 1.8, ((0, 4), (1, 32)), jnp.float32),
        "normals": gaussian(key_of[2], (SWEEPS, K, M), 1.0, 6.0, ((1, 4), (2, 32)), jnp.float32),
        "block_len": uneven_parts(key_of[3], NB, LIVE, BMAX, 1).astype(jnp.int32),
        "scale_start": jnp.clip(jnp.exp(math.log(5.0) - 3.218876 * jax.random.uniform(key_of[4], (M,), jnp.float32) ** shard_levels(key_of[4], (M,), ((0, 32),), -0.2, 0.2)), 0.2, 5.0),
        "ancestry_weight": jnp.clip(jnp.exp(jax.random.uniform(key_of[5], (K,), jnp.float32, math.log(4.0), math.log(64.0))), 4.0, 64.0),
        "dosage": jnp.clip(2.0 * jax.random.uniform(key_of[6], (SAMPLES, M), jnp.float32) ** shard_levels(key_of[6], (SAMPLES, M), ((0, 32), (1, 4)), -0.2, 0.2), 0.0, 2.0).astype(jnp.bfloat16),
    }


shape_total = 1.5
global_shrink = 0.01

def live_mask(block_len):
    position = jnp.arange(BMAX, dtype=jnp.int32)
    return (position[None, :] < block_len[:, None]).astype(jnp.float32)

def solve_block(ld_block, live_rows, inverse, targets, normals, noise_level):
    correlation = ld_block.astype(jnp.float32) * (live_rows[:, None] * live_rows[None, :])
    system = correlation + jnp.diag(live_rows * inverse + (1.0 - live_rows))
    factor = jnp.linalg.cholesky(system)
    forward = lax.linalg.triangular_solve(factor, targets[:, None], left_side=True, lower=True)[:, 0]
    forward = forward + noise_level * normals * live_rows
    effect = lax.linalg.triangular_solve(factor, forward[:, None], left_side=True, lower=True, transpose_a=True)[:, 0]
    fitted = jnp.dot(correlation, effect, precision=lax.Precision.HIGHEST)
    misfit = targets - fitted
    return (effect, jnp.sum(misfit * misfit), jnp.sum(effect * effect * inverse * live_rows))

def reference(ld_blocks, marginal, normals, block_len, scale_start, ancestry_weight, dosage):
    live_rows = live_mask(block_len)
    live_total = jnp.sum(live_rows)
    shrink = scale_start.reshape(NB, BMAX)
    shrink_rate = shape_total / (shrink + global_shrink)
    variance = jnp.ones((K,), jnp.float32)
    drawn = []
    for sweep_index in range(SWEEPS):
        inverse = 1.0 / shrink
        new_effects = []
        new_variance = []
        for ancestry in range(K):
            noise_level = jnp.sqrt(variance[ancestry] / ancestry_weight[ancestry])
            targets = marginal[ancestry].reshape(NB, BMAX) * live_rows

            def one_block(items):
                return solve_block(items[0], items[1], items[2], items[3], items[4], noise_level)
            effect, misfit, penalty = lax.map(one_block, (ld_blocks[ancestry], live_rows, inverse, targets, normals[sweep_index, ancestry].reshape(NB, BMAX)))
            new_effects.append(effect)
            new_variance.append((jnp.sum(misfit) + jnp.sum(penalty) + 1.0) / (live_total + 1.0))
        pooled = jnp.zeros((NB, BMAX), jnp.float32)
        for ancestry in range(K):
            pooled = pooled + ancestry_weight[ancestry] * new_effects[ancestry] * new_effects[ancestry] / new_variance[ancestry]
        shrink = (pooled + 1.0) / (2.0 + jnp.sqrt(4.0 + 2.0 * shrink_rate * (pooled + 1.0)))
        shrink_rate = shape_total / (shrink + global_shrink)
        variance = jnp.stack(new_variance)
        drawn.append(jnp.stack(new_effects).reshape(K, NB * BMAX))
    total = drawn[0]
    for sweep_index in range(1, SWEEPS):
        total = total + drawn[sweep_index]
    effects = total / SWEEPS
    weights = effects.astype(jnp.bfloat16)
    ordered = weights.reshape(K, N_SAMP, N_SLAB, QUART).transpose(0, 2, 1, 3).reshape(K, NB * BMAX)
    products = jnp.dot(dosage.astype(jnp.float32), ordered.T.astype(jnp.float32), preferred_element_type=jnp.float32)
    scores = (products - lax.optimization_barrier(jnp.sum(ordered.astype(jnp.float32), axis=1))[None, :]) / jnp.sqrt(live_total)
    return (effects, shrink.reshape(NB * BMAX), scores)
```

```python
import functools

import jax
import jax.numpy as jnp
from jax import lax
from jax.experimental import pallas as pl
from jax.experimental.pallas import tpu as pltpu
from jax.sharding import PartitionSpec as P

SWEEPS = 2
TILE = 128
STEP = 8

shape_total = 1.5
global_shrink = 0.01

MESH = pl.DeviceIdType.MESH
F32 = jnp.float32
BF16 = jnp.bfloat16


def split3(x):
    high = x.astype(BF16)
    rest = x - high.astype(F32)
    mid = rest.astype(BF16)
    low = (rest - mid.astype(F32)).astype(BF16)
    return high, mid, low


def left_terms(x):
    high, mid, low = split3(x)
    return jnp.concatenate([high, high, mid, mid, high, low], axis=1)


def right_terms(x):
    high, mid, low = split3(x)
    return jnp.concatenate([high, mid, high, mid, low, high], axis=0)


def lane_spread(x, column):
    index = jnp.full(x.shape, column, jnp.int32)
    return jnp.take_along_axis(x, index, axis=1, mode="promise_in_bounds")


def row_spread(x, row):
    return jnp.broadcast_to(x[row : row + 1, :], x.shape)


def eliminate(slots, diag, pivots):
    lane = lax.broadcasted_iota(jnp.int32, (STEP, TILE), 1)
    sub = lax.broadcasted_iota(jnp.int32, (STEP, TILE), 0)
    for step in range(TILE // STEP):
        first = step * STEP
        rows = pl.ds(first, STEP)
        value = [diag[b, rows, :] for b in range(slots)]
        columns = [[None] * STEP for _ in range(slots)]
        for j in range(STEP):
            for b in range(slots):
                columns[b][j] = lane_spread(value[b], first + j)
        held = list(value)
        inverse = list(value)
        for j in range(STEP):
            for b in range(slots):
                column = columns[b]
                pivot = 1.0 / row_spread(column[j], j)
                unit = jnp.where(sub == j, 1.0, 0.0)
                v = jnp.where(lane == first + j, unit, value[b])
                held[b] = jnp.where(sub == j, v, held[b])
                inverse[b] = jnp.where(sub == j, pivot, inverse[b])
                factor = jnp.where(sub == j, 0.0, column[j]) * pivot
                value[b] = v - factor * row_spread(v, j)
                for k in range(j + 1, STEP):
                    column[k] = column[k] - factor * row_spread(column[k], j)
        solved = []
        for b in range(slots):
            whole = value[b] * inverse[b]
            diag[b, rows, :] = held[b]
            pivots[b, rows, :] = inverse[b]
            solved.append([row_spread(whole, j) for j in range(STEP)])
        inside = (lane >= first) & (lane < first + STEP)
        later = range(step + 1, TILE // STEP)
        below = {}
        total = {}
        for k in later:
            for b in range(slots):
                below[b, k] = diag[b, pl.ds(k * STEP, STEP), :]
                total[b, k] = jnp.where(inside, 0.0, below[b, k])
        for j in range(STEP):
            for k in later:
                for b in range(slots):
                    total[b, k] = total[b, k] - lane_spread(below[b, k], first + j) * solved[b][j]
        for k in later:
            for b in range(slots):
                diag[b, pl.ds(k * STEP, STEP), :] = total[b, k]


def solve_kernel(slots, size, length, ld, marginal, normals, shrink, noise, effect, stats,
                 work, diag, pivots, rhs, panel):
    tiles = size // TILE
    row = lax.broadcasted_iota(jnp.int32, (TILE, TILE), 0)
    col = lax.broadcasted_iota(jnp.int32, (TILE, TILE), 1)
    wide = lax.broadcasted_iota(jnp.int32, (1, size), 1)
    wide_rows = lax.broadcasted_iota(jnp.int32, (TILE, size), 1)
    noise_level = noise[0:1, 0:1]

    def of_slot(ref, b):
        return ref[0:1, b * size : (b + 1) * size]

    for b in range(slots):
        live = (wide < length[b]).astype(F32)
        extra = live / of_slot(shrink, b) + (1.0 - live)

        def build(r, carry, b=b, live=live, extra=extra):
            rows = pl.ds(pl.multiple_of(r * TILE, TILE), TILE)
            tile_row = lax.broadcasted_iota(jnp.int32, (TILE, 1), 0) + r * TILE
            full_row = lax.broadcasted_iota(jnp.int32, (TILE, size), 0) + r * TILE
            inside = (full_row < length[b]) & (wide_rows < length[b])
            value = jnp.where(inside, ld[b, rows, :].astype(F32), 0.0)
            work[b, rows, :] = value + jnp.where(full_row == wide_rows, extra, 0.0)
            return carry

        lax.fori_loop(0, tiles, build, 0)

    def one_panel(p, totals):
        start = pl.multiple_of(p * TILE, TILE)
        here = pl.ds(start, TILE)
        for b in range(slots):
            diag[b] = work[b, here, here]
        eliminate(slots, diag, pivots)
        result = []
        for b in range(slots):
            lower = jnp.where(col <= row, diag[b], 0.0)
            work[b, here, here] = jnp.where(col == row, 1.0, 0.0)
            rhs[...] = right_terms(work[b, here, :])
            rows = jnp.dot(left_terms(lower), rhs[...], preferred_element_type=F32)
            panel[b] = rows
            inverse = pivots[b]
            inverse_wide = jnp.concatenate([inverse] * tiles, axis=1)
            rhs[...] = right_terms(rows * inverse_wide)

            def below(k, carry, b=b):
                below_rows = pl.ds(pl.multiple_of(k * TILE, TILE), TILE)
                across = panel[b, :, below_rows].T
                change = jnp.dot(left_terms(across), rhs[...], preferred_element_type=F32)
                kept = work[b, below_rows, :]
                gone = (wide_rows >= start) & (wide_rows < start + TILE)
                work[b, below_rows, :] = jnp.where(gone, 0.0, kept) - change
                return carry

            lax.fori_loop(p + 1, tiles, below, 0)
            reach = wide < start + TILE
            live = wide < length[b]
            target = jnp.where(reach & live, of_slot(marginal, b), 0.0)
            forward = jnp.sum(rows * target, axis=1, keepdims=True)
            own = pl.ds(pl.multiple_of(b * size + p * TILE, TILE), TILE)
            own_live = (lax.broadcasted_iota(jnp.int32, (1, TILE), 1) + start) < length[b]
            draw = jnp.where(own_live, normals[0:1, own], 0.0)
            draw = jnp.broadcast_to(draw, (TILE, TILE)).T
            weight = forward * inverse + noise_level * draw * jnp.sqrt(inverse)
            weight_wide = jnp.concatenate([weight] * tiles, axis=1)
            part = jnp.sum(rows * weight_wide, axis=0, keepdims=True)
            result.append(totals[b] + jnp.where(reach, part, 0.0))
        return tuple(result)

    totals = lax.fori_loop(0, tiles, one_panel, tuple(jnp.zeros((1, size), F32) for _ in range(slots)))
    squares = jnp.zeros((1, size), F32)
    count = jnp.zeros((1, size), F32)
    for b in range(slots):
        live = (wide < length[b]).astype(F32)
        value = totals[b] * live
        effect[0:1, b * size : (b + 1) * size] = value
        high, mid, low = split3(value)
        pad = jnp.zeros((5, size), BF16)
        parts = jnp.concatenate([high.astype(F32), mid.astype(F32), low.astype(F32), pad.astype(F32)], axis=0)
        fitted = jnp.dot(parts.astype(BF16), ld[b], preferred_element_type=F32)
        fitted = jnp.sum(fitted, axis=0, keepdims=True)
        misfit = (of_slot(marginal, b) - fitted) * live
        squares = squares + misfit * misfit + value * value * live / of_slot(shrink, b)
        count = count + live
    lane = lax.broadcasted_iota(jnp.int32, (1, TILE), 1)
    stats[...] = jnp.where(lane == 0, jnp.sum(squares), jnp.where(lane == 1, jnp.sum(count), 0.0))


def solve(block_len, ld, marginal, normals, shrink, noise):
    slots, size = ld.shape[0], ld.shape[1]
    vmem = pl.BlockSpec(memory_space=pltpu.VMEM)
    return pl.pallas_call(
        functools.partial(solve_kernel, slots, size),
        out_shape=(
            jax.ShapeDtypeStruct((1, slots * size), F32),
            jax.ShapeDtypeStruct((1, TILE), F32),
        ),
        in_specs=[pl.BlockSpec(memory_space=pltpu.SMEM)] + [vmem] * 5,
        out_specs=(vmem, vmem),
        scratch_shapes=[
            pltpu.VMEM((slots, size, size), F32),
            pltpu.VMEM((slots, TILE, TILE), F32),
            pltpu.VMEM((slots, TILE, TILE), F32),
            pltpu.VMEM((6 * TILE, size), BF16),
            pltpu.VMEM((slots, TILE, size), F32),
        ],
        name="solve",
    )(block_len, ld, marginal, normals, shrink, noise)


def enter(samp, slab, others_samp, others_slab):
    me, my = lax.axis_index("samp"), lax.axis_index("slab")
    barrier = pltpu.get_barrier_semaphore()

    def greet(d, carry):
        peer = lax.rem(me + d, samp)
        pl.semaphore_signal(barrier, inc=1, device_id=(peer, my), device_id_type=MESH)
        return carry

    lax.fori_loop(1, samp, greet, 0)
    for d in range(1, slab):
        peer = lax.rem(my + d, slab)
        pl.semaphore_signal(barrier, inc=1, device_id=(me, peer), device_id_type=MESH)
    pl.semaphore_wait(barrier, samp - 1 + slab - 1)
    return me, my


def sums_of(gathered, slab):
    total = jnp.sum(gathered, axis=0)
    return [total[k : k + 1, :] for k in range(slab)]


def pooled_shrink(totals, effects, weights, shrink, rate):
    pooled = jnp.zeros_like(shrink)
    for k, total in enumerate(totals):
        variance = (total[0:1, 0:1] + 1.0) / (total[0:1, 1:2] + 1.0)
        effect = effects[k]
        pooled = pooled + weights[0:1, k : k + 1] * effect * effect / variance
    new = (pooled + 1.0) / (2.0 + jnp.sqrt(4.0 + 2.0 * rate * (pooled + 1.0)))
    return new


def share_kernel(samp, slab, effect, stats, weights, shrink, new_shrink, noise,
                 effects, own_stats, gathered, e_send, e_recv, s_send, s_recv, g_send, g_recv, local):
    me, my = enter(samp, slab, None, None)
    keep = [
        pltpu.make_async_copy(effect, effects.at[my], local.at[0]),
        pltpu.make_async_copy(stats, own_stats.at[my], local.at[1]),
    ]
    for copy in keep:
        copy.start()
    stat_copies, effect_copies = [], []
    for d in range(1, slab):
        peer = lax.rem(my + d, slab)
        stat_copies.append(pltpu.make_async_remote_copy(
            stats, own_stats.at[my], s_send.at[d], s_recv.at[d], device_id=(me, peer), device_id_type=MESH))
        stat_copies[-1].start()
    for d in range(1, slab):
        peer = lax.rem(my + d, slab)
        effect_copies.append(pltpu.make_async_remote_copy(
            effect, effects.at[my], e_send.at[d], e_recv.at[d], device_id=(me, peer), device_id_type=MESH))
        effect_copies[-1].start()
    for copy in keep:
        copy.wait()
    for copy in stat_copies:
        copy.wait()
    mine = pltpu.make_async_copy(own_stats, gathered.at[me], local.at[0])
    mine.start()

    def spread(d):
        peer = lax.rem(me + d, samp)
        return pltpu.make_async_remote_copy(
            own_stats, gathered.at[me], g_send.at[d], g_recv.at[d], device_id=(peer, my), device_id_type=MESH)

    def start(d, carry):
        spread(d).start()
        return carry

    def finish(d, carry):
        spread(d).wait()
        return carry

    lax.fori_loop(1, samp, start, 0)
    for copy in effect_copies:
        copy.wait()
    lax.fori_loop(1, samp, finish, 0)
    mine.wait()
    totals = sums_of(gathered[:, :, 0, :], slab)
    old = shrink[...]
    rate = shape_total / (old + global_shrink)
    new_shrink[...] = pooled_shrink(totals, [effects[k] for k in range(slab)], weights, old, rate)
    lane = lax.broadcasted_iota(jnp.int32, (1, TILE), 1)
    level = jnp.zeros((1, TILE), F32)
    for k, total in enumerate(totals):
        variance = (total[0:1, 0:1] + 1.0) / (total[0:1, 1:2] + 1.0)
        own = jnp.sqrt(variance / weights[0:1, k : k + 1])
        level = jnp.where(my == k, jnp.broadcast_to(own, (1, TILE)), level)
    noise[...] = level


def share(samp, slab, effect, stats, weights, shrink):
    width = effect.shape[1]
    vmem = pl.BlockSpec(memory_space=pltpu.VMEM)
    dma = pltpu.SemaphoreType.DMA
    return pl.pallas_call(
        functools.partial(share_kernel, samp, slab),
        out_shape=(
            jax.ShapeDtypeStruct((1, width), F32),
            jax.ShapeDtypeStruct((1, TILE), F32),
        ),
        in_specs=[vmem] * 4,
        out_specs=(vmem, vmem),
        scratch_shapes=[
            pltpu.VMEM((slab, 1, width), F32),
            pltpu.VMEM((slab, 1, TILE), F32),
            pltpu.VMEM((samp, slab, 1, TILE), F32),
            dma((slab,)), dma((slab,)), dma((slab,)), dma((slab,)), dma((samp,)), dma((samp,)), dma((2,)),
        ],
        compiler_params=pltpu.CompilerParams(collective_id=0, has_side_effects=True),
        name="share",
    )(effect, stats, weights, shrink)


def finish_kernel(samp, slab, effect, stats, weights, shrink, rate, quarters, dosage, new_shrink, scores,
                  effects, own_stats, gathered, own_quarter, columns, spread_columns, dose, partial, parts,
                  e_send, e_recv, s_send, s_recv, q_send, q_recv, g_send, g_recv, w_send, w_recv,
                  p_send, p_recv, local):
    chunks = quarters.shape[1]
    fetch = pltpu.make_async_copy(dosage, dose, local.at[3])
    fetch.start()
    me, my = enter(samp, slab, None, None)
    keep = [
        pltpu.make_async_copy(effect, effects.at[my], local.at[0]),
        pltpu.make_async_copy(stats, own_stats.at[my], local.at[1]),
        pltpu.make_async_copy(quarters.at[my], own_quarter.at[my], local.at[2]),
    ]
    for copy in keep:
        copy.start()
    first, second = [], []
    for d in range(1, slab):
        peer = lax.rem(my + d, slab)
        to = dict(device_id=(me, peer), device_id_type=MESH)
        first.append(pltpu.make_async_remote_copy(
            quarters.at[peer], own_quarter.at[my], q_send.at[d], q_recv.at[d], **to))
        first[-1].start()
        first.append(pltpu.make_async_remote_copy(stats, own_stats.at[my], s_send.at[d], s_recv.at[d], **to))
        first[-1].start()
    for d in range(1, slab):
        peer = lax.rem(my + d, slab)
        to = dict(device_id=(me, peer), device_id_type=MESH)
        second.append(pltpu.make_async_remote_copy(effect, effects.at[my], e_send.at[d], e_recv.at[d], **to))
        second[-1].start()
    for copy in keep + first:
        copy.wait()
    mine = [
        pltpu.make_async_copy(own_stats, gathered.at[me], local.at[0]),
        pltpu.make_async_copy(own_quarter, columns.at[me], local.at[1]),
    ]
    for copy in mine:
        copy.start()

    def spread(d):
        peer = lax.rem(me + d, samp)
        to = dict(device_id=(peer, my), device_id_type=MESH)
        return (
            pltpu.make_async_remote_copy(own_quarter, columns.at[me], w_send.at[d], w_recv.at[d], **to),
            pltpu.make_async_remote_copy(own_stats, gathered.at[me], g_send.at[d], g_recv.at[d], **to),
        )

    def start(d, carry):
        for copy in spread(d):
            copy.start()
        return carry

    def finish(d, carry):
        for copy in spread(d):
            copy.wait()
        return carry

    lax.fori_loop(1, samp, start, 0)
    for copy in second:
        copy.wait()
    lax.fori_loop(1, samp, finish, 0)
    for copy in mine:
        copy.wait()
    fetch.wait()

    def arrange(g, sums):
        for c in range(chunks):
            value = jnp.concatenate(
                [columns[g, k, pl.ds(c, 1), :] for k in range(slab)] + [jnp.zeros((16 - slab, TILE), F32)], axis=0)
            at = pl.ds(pl.multiple_of((g * chunks + c) * TILE, TILE), TILE)
            value = value.astype(BF16)
            spread_columns[:, at] = value
            sums = sums + value.astype(F32)
        return sums

    sums = lax.fori_loop(0, samp, arrange, jnp.zeros((16, TILE), F32))
    products = lax.dot_general(
        spread_columns[...], dose[...], (((1,), (1,)), ((), ())), preferred_element_type=F32)
    totals = sums_of(gathered[:, :, 0, :], slab)
    part = products - jnp.sum(sums, axis=1, keepdims=True)
    for k in range(slab):
        partial[k] = part[k : k + 1, :]
    last = []
    for d in range(1, slab):
        peer = lax.rem(my + d, slab)
        last.append(pltpu.make_async_remote_copy(
            partial.at[peer], parts.at[my], p_send.at[d], p_recv.at[d], device_id=(me, peer), device_id_type=MESH))
        last[-1].start()
    home = pltpu.make_async_copy(partial.at[my], parts.at[my], local.at[2])
    home.start()
    new_shrink[...] = pooled_shrink(
        totals, [effects[k] for k in range(slab)], weights, shrink[...], rate[...])
    for copy in last:
        copy.wait()
    home.wait()
    total = parts[0]
    for k in range(1, slab):
        total = total + parts[k]
    scores[...] = total / jnp.sqrt(totals[0][0:1, 1:2])


def finish(samp, slab, effect, stats, weights, shrink, rate, quarters, dosage):
    width = effect.shape[1]
    rows = dosage.shape[0]
    vmem = pl.BlockSpec(memory_space=pltpu.VMEM)
    dma = pltpu.SemaphoreType.DMA
    return pl.pallas_call(
        functools.partial(finish_kernel, samp, slab),
        out_shape=(
            jax.ShapeDtypeStruct((1, width), F32),
            jax.ShapeDtypeStruct((1, rows), F32),
        ),
        in_specs=[vmem] * 6 + [pl.BlockSpec(memory_space=pl.ANY)],
        out_specs=(vmem, vmem),
        scratch_shapes=[
            pltpu.VMEM((slab, 1, width), F32),
            pltpu.VMEM((slab, 1, TILE), F32),
            pltpu.VMEM((samp, slab, 1, TILE), F32),
            pltpu.VMEM(quarters.shape, F32),
            pltpu.VMEM((samp, *quarters.shape), F32),
            pltpu.VMEM((16, dosage.shape[1]), BF16),
            pltpu.VMEM(dosage.shape, BF16),
            pltpu.VMEM((slab, 1, rows), F32),
            pltpu.VMEM((slab, 1, rows), F32),
            dma((slab,)), dma((slab,)), dma((slab,)), dma((slab,)), dma((slab,)), dma((slab,)),
            dma((samp,)), dma((samp,)), dma((samp,)), dma((samp,)),
            dma((slab,)), dma((slab,)), dma((4,)),
        ],
        compiler_params=pltpu.CompilerParams(collective_id=1, has_side_effects=True),
        name="finish",
    )(effect, stats, weights, shrink, rate, quarters, dosage)


def per_device(samp, slab, ld_blocks, marginal, normals, block_len, scale_start, ancestry_weight, dosage):
    width = marginal.shape[1]
    own_weight = lax.dynamic_index_in_dim(ancestry_weight, lax.axis_index("slab"), 0, keepdims=False)
    weights = ancestry_weight.reshape(1, slab)
    weights = jnp.pad(weights, ((0, 0), (0, TILE - slab)))
    shrink = scale_start.reshape(1, width)
    noise = jnp.full((1, TILE), jnp.sqrt(1.0 / own_weight), F32)
    effect0, stats0 = solve(block_len, ld_blocks[0], marginal, normals[0], shrink, noise)
    shrink1, noise1 = share(samp, slab, effect0, stats0, weights, shrink)
    effect1, stats1 = solve(block_len, ld_blocks[0], marginal, normals[1], shrink1, noise1)
    effects = (effect0 + effect1) / SWEEPS
    quarters = effects.reshape(slab, width // slab // TILE, TILE)
    rate1 = shape_total / (shrink1 + global_shrink)
    shrink2, scores = finish(samp, slab, effect1, stats1, weights, shrink1, rate1, quarters, dosage)
    return (effects, shrink2.reshape(width), scores.reshape(-1, 1))


def solution(mesh):
    return jax.shard_map(
        functools.partial(per_device, mesh.shape["samp"], mesh.shape["slab"]),
        mesh=mesh,
        in_specs=(
            P("slab", "samp", None, None),
            P("slab", "samp"),
            P(None, "slab", "samp"),
            P("samp"),
            P("samp"),
            P(),
            P("samp", "slab"),
        ),
        out_specs=(P("slab", "samp"), P("samp"), P("samp", "slab")),
        check_vma=False,
    )
```

```python
import functools

import jax
import jax.numpy as jnp
from jax import lax
from jax.experimental import pallas as pl
from jax.experimental.pallas import tpu as pltpu
from jax.sharding import PartitionSpec as P

SWEEPS = 2
TILE = 128
STEP = 8

shape_total = 1.5
global_shrink = 0.01

MESH = pl.DeviceIdType.MESH
F32 = jnp.float32
BF16 = jnp.bfloat16


def split3(x):
    high = x.astype(BF16)
    rest = x - high.astype(F32)
    mid = rest.astype(BF16)
    low = (rest - mid.astype(F32)).astype(BF16)
    return high, mid, low


def left_terms(x):
    high, mid, low = split3(x)
    return jnp.concatenate([high, high, mid, mid, high, low], axis=1)


def right_terms(x):
    high, mid, low = split3(x)
    return jnp.concatenate([high, mid, high, mid, low, high], axis=0)


def lane_spread(x, column):
    index = jnp.full(x.shape, column, jnp.int32)
    return jnp.take_along_axis(x, index, axis=1, mode="promise_in_bounds")


def row_spread(x, row):
    return jnp.broadcast_to(x[row : row + 1, :], x.shape)


def eliminate(slots, diag, pivots):
    lane = lax.broadcasted_iota(jnp.int32, (STEP, TILE), 1)
    sub = lax.broadcasted_iota(jnp.int32, (STEP, TILE), 0)
    for step in range(TILE // STEP):
        first = step * STEP
        rows = pl.ds(first, STEP)
        value = [diag[b, rows, :] for b in range(slots)]
        columns = [[None] * STEP for _ in range(slots)]
        for j in range(STEP):
            for b in range(slots):
                columns[b][j] = lane_spread(value[b], first + j)
        held = list(value)
        inverse = list(value)
        for j in range(STEP):
            for b in range(slots):
                column = columns[b]
                pivot = 1.0 / row_spread(column[j], j)
                unit = jnp.where(sub == j, 1.0, 0.0)
                v = jnp.where(lane == first + j, unit, value[b])
                held[b] = jnp.where(sub == j, v, held[b])
                inverse[b] = jnp.where(sub == j, pivot, inverse[b])
                factor = jnp.where(sub == j, 0.0, column[j]) * pivot
                value[b] = v - factor * row_spread(v, j)
                for k in range(j + 1, STEP):
                    column[k] = column[k] - factor * row_spread(column[k], j)
        solved = []
        for b in range(slots):
            whole = value[b] * inverse[b]
            diag[b, rows, :] = held[b]
            pivots[b, rows, :] = inverse[b]
            solved.append([row_spread(whole, j) for j in range(STEP)])
        inside = (lane >= first) & (lane < first + STEP)
        later = range(step + 1, TILE // STEP)
        below = {}
        total = {}
        for k in later:
            for b in range(slots):
                below[b, k] = diag[b, pl.ds(k * STEP, STEP), :]
                total[b, k] = jnp.where(inside, 0.0, below[b, k])
        for j in range(STEP):
            for k in later:
                for b in range(slots):
                    total[b, k] = total[b, k] - lane_spread(below[b, k], first + j) * solved[b][j]
        for k in later:
            for b in range(slots):
                diag[b, pl.ds(k * STEP, STEP), :] = total[b, k]


def of_slot(value, b, size):
    return value[0:1, b * size : (b + 1) * size]


def solve(slots, size, length, ld, marginal, normals, shrink, noise_level, work, diag, pivots, rhs, panel):
    tiles = size // TILE
    row = lax.broadcasted_iota(jnp.int32, (TILE, TILE), 0)
    col = lax.broadcasted_iota(jnp.int32, (TILE, TILE), 1)
    wide = lax.broadcasted_iota(jnp.int32, (1, size), 1)
    wide_rows = lax.broadcasted_iota(jnp.int32, (TILE, size), 1)

    for b in range(slots):
        live = (wide < length[b]).astype(F32)
        extra = live / of_slot(shrink, b, size) + (1.0 - live)

        def build(r, carry, b=b, extra=extra):
            rows = pl.ds(pl.multiple_of(r * TILE, TILE), TILE)
            full_row = lax.broadcasted_iota(jnp.int32, (TILE, size), 0) + r * TILE
            inside = (full_row < length[b]) & (wide_rows < length[b])
            value = jnp.where(inside, ld[b, rows, :].astype(F32), 0.0)
            work[b, rows, :] = value + jnp.where(full_row == wide_rows, extra, 0.0)
            return carry

        lax.fori_loop(0, tiles, build, 0)

    def one_panel(p, totals):
        start = pl.multiple_of(p * TILE, TILE)
        here = pl.ds(start, TILE)
        for b in range(slots):
            diag[b] = work[b, here, here]
        eliminate(slots, diag, pivots)
        result = []
        for b in range(slots):
            lower = jnp.where(col <= row, diag[b], 0.0)
            work[b, here, here] = jnp.where(col == row, 1.0, 0.0)
            rhs[...] = right_terms(work[b, here, :])
            rows = jnp.dot(left_terms(lower), rhs[...], preferred_element_type=F32)
            panel[b] = rows
            inverse = pivots[b]
            inverse_wide = jnp.concatenate([inverse] * tiles, axis=1)
            rhs[...] = right_terms(rows * inverse_wide)

            def below(k, carry, b=b):
                below_rows = pl.ds(pl.multiple_of(k * TILE, TILE), TILE)
                across = panel[b, :, below_rows].T
                change = jnp.dot(left_terms(across), rhs[...], preferred_element_type=F32)
                kept = work[b, below_rows, :]
                gone = (wide_rows >= start) & (wide_rows < start + TILE)
                work[b, below_rows, :] = jnp.where(gone, 0.0, kept) - change
                return carry

            lax.fori_loop(p + 1, tiles, below, 0)
            reach = wide < start + TILE
            live = wide < length[b]
            target = jnp.where(reach & live, marginal[0:1, b * size : (b + 1) * size], 0.0)
            forward = jnp.sum(rows * target, axis=1, keepdims=True)
            own = pl.ds(pl.multiple_of(b * size + p * TILE, TILE), TILE)
            own_live = (lax.broadcasted_iota(jnp.int32, (1, TILE), 1) + start) < length[b]
            draw = jnp.where(own_live, normals[0:1, own], 0.0)
            draw = jnp.broadcast_to(draw, (TILE, TILE)).T
            weight = forward * inverse + noise_level * draw * jnp.sqrt(inverse)
            weight_wide = jnp.concatenate([weight] * tiles, axis=1)
            part = jnp.sum(rows * weight_wide, axis=0, keepdims=True)
            result.append(totals[b] + jnp.where(reach, part, 0.0))
        return tuple(result)

    totals = lax.fori_loop(0, tiles, one_panel, tuple(jnp.zeros((1, size), F32) for _ in range(slots)))
    squares = jnp.zeros((1, size), F32)
    count = jnp.zeros((1, size), F32)
    drawn = []
    for b in range(slots):
        live = (wide < length[b]).astype(F32)
        value = totals[b] * live
        drawn.append(value)
        high, mid, low = split3(value)
        parts = jnp.concatenate([high.astype(F32), mid.astype(F32), low.astype(F32), jnp.zeros((5, size), F32)], axis=0)
        fitted = jnp.dot(parts.astype(BF16), ld[b], preferred_element_type=F32)
        fitted = jnp.sum(fitted, axis=0, keepdims=True)
        misfit = (marginal[0:1, b * size : (b + 1) * size] - fitted) * live
        squares = squares + misfit * misfit + value * value * live / of_slot(shrink, b, size)
        count = count + live
    lane = lax.broadcasted_iota(jnp.int32, (1, TILE), 1)
    stats = jnp.where(lane == 0, jnp.sum(squares), jnp.where(lane == 1, jnp.sum(count), 0.0))
    return jnp.concatenate(drawn, axis=1), stats


def variances_of(gathered, slab):
    total = jnp.sum(gathered[:, :, 0, :], axis=0)
    rows = [total[k : k + 1, :] for k in range(slab)]
    return [(r[0:1, 0:1] + 1.0) / (r[0:1, 1:2] + 1.0) for r in rows], rows[0][0:1, 1:2]


def next_shrink(variances, effects, weights, shrink):
    rate = shape_total / (shrink + global_shrink)
    pooled = jnp.zeros_like(shrink)
    for k, variance in enumerate(variances):
        effect = effects[k]
        pooled = pooled + weights[k] * effect * effect / variance
    return (pooled + 1.0) / (2.0 + jnp.sqrt(4.0 + 2.0 * rate * (pooled + 1.0)))


def whole_kernel(samp, slab, slots, size, length, weights_ref, ld, marginal, normals, scale, dosage,
                 mean, new_shrink, scores,
                 work, diag, pivots, rhs, panel, drawn, stats, effects, own_stats, gathered,
                 quarters, columns, spread_columns, dose, partial, parts,
                 e_send, e_recv, s_send, s_recv, g_send, g_recv, q_send, q_recv, w_send, w_recv, p_send, p_recv, local):
    me, my = lax.axis_index("samp"), lax.axis_index("slab")
    width = slots * size
    quarter = width // slab
    barrier = pltpu.get_barrier_semaphore()

    def greet(d, carry):
        pl.semaphore_signal(barrier, inc=1, device_id=(lax.rem(me + d, samp), my), device_id_type=MESH)
        return carry

    lax.fori_loop(1, samp, greet, 0)
    for d in range(1, slab):
        pl.semaphore_signal(barrier, inc=1, device_id=(me, lax.rem(my + d, slab)), device_id_type=MESH)
    fetch = pltpu.make_async_copy(dosage, dose, local.at[0])
    fetch.start()
    weights = [weights_ref[k] for k in range(slab)]
    own_weight = weights[0]
    for k in range(1, slab):
        own_weight = jnp.where(my == k, weights[k], own_weight)
    shrink = scale[...].reshape(1, width)

    def near(d):
        return dict(device_id=(me, lax.rem(my + d, slab)), device_id_type=MESH)

    def far(d):
        return dict(device_id=(lax.rem(me + d, samp), my), device_id_type=MESH)

    def run(copies):
        for copy in copies:
            copy.start()
        return copies

    def wait(copies):
        for copy in copies:
            copy.wait()

    variance = jnp.ones((1, 1), F32)
    for s in range(SWEEPS):
        noise_level = jnp.sqrt(variance / own_weight)
        effect, stat = solve(slots, size, length, ld, marginal, normals.at[s], shrink, noise_level,
                             work, diag, pivots, rhs, panel)
        drawn[s] = effect
        if s == SWEEPS - 1:
            total = drawn[0]
            for r in range(1, SWEEPS):
                total = total + drawn[r]
            mean[...] = total / SWEEPS
        stats[s] = stat
        if s == 0:
            pl.semaphore_wait(barrier, samp - 1 + slab - 1)
        first = [pltpu.make_async_copy(stats.at[s], own_stats.at[s, my], local.at[1])]
        if s == SWEEPS - 1:
            own = pl.ds(pl.multiple_of(my * quarter, TILE), quarter)
            first.append(pltpu.make_async_copy(mean.at[:, own], quarters.at[my], local.at[3]))
        for d in range(1, slab):
            first.append(pltpu.make_async_remote_copy(
                stats.at[s], own_stats.at[s, my], s_send.at[s, d], s_recv.at[s, d], **near(d)))
            if s == SWEEPS - 1:
                theirs = pl.ds(pl.multiple_of(lax.rem(my + d, slab) * quarter, TILE), quarter)
                first.append(pltpu.make_async_remote_copy(
                    mean.at[:, theirs], quarters.at[my], q_send.at[d], q_recv.at[d], **near(d)))
        run(first)
        second = [pltpu.make_async_copy(drawn.at[s], effects.at[s, my], local.at[2])]
        for d in range(1, slab):
            second.append(pltpu.make_async_remote_copy(
                drawn.at[s], effects.at[s, my], e_send.at[s, d], e_recv.at[s, d], **near(d)))
        run(second)
        wait(first)
        mine = [pltpu.make_async_copy(own_stats.at[s], gathered.at[s, me], local.at[1])]
        if s == SWEEPS - 1:
            mine.append(pltpu.make_async_copy(quarters, columns.at[me], local.at[3]))
        run(mine)

        def spread(d, s=s):
            copies = [pltpu.make_async_remote_copy(
                own_stats.at[s], gathered.at[s, me], g_send.at[s, d], g_recv.at[s, d], **far(d))]
            if s == SWEEPS - 1:
                copies.append(pltpu.make_async_remote_copy(
                    quarters, columns.at[me], w_send.at[d], w_recv.at[d], **far(d)))
            return copies

        def start(d, carry, spread=spread):
            run(spread(d))
            return carry

        def finish(d, carry, spread=spread):
            wait(spread(d))
            return carry

        lax.fori_loop(1, samp, start, 0)
        wait(second)
        lax.fori_loop(1, samp, finish, 0)
        wait(mine)
        variances, live_total = variances_of(gathered[s], slab)
        if s < SWEEPS - 1:
            shrink = next_shrink(variances, [effects[s, k] for k in range(slab)], weights, shrink)
            variance = variances[0]
            for k in range(1, slab):
                variance = jnp.where(my == k, variances[k], variance)
    fetch.wait()
    chunks = quarter // TILE

    def arrange(g, sums):
        for c in range(chunks):
            value = jnp.concatenate(
                [columns[g, k, :, pl.ds(c * TILE, TILE)] for k in range(slab)] + [jnp.zeros((16 - slab, TILE), F32)], axis=0)
            at = pl.ds(pl.multiple_of((g * chunks + c) * TILE, TILE), TILE)
            value = value.astype(BF16)
            spread_columns[:, at] = value
            sums = sums + value.astype(F32)
        return sums

    sums = lax.fori_loop(0, samp, arrange, jnp.zeros((16, TILE), F32))
    products = lax.dot_general(
        spread_columns[...], dose[...], (((1,), (1,)), ((), ())), preferred_element_type=F32)
    part = products - jnp.sum(sums, axis=1, keepdims=True)
    for k in range(slab):
        partial[k] = part[k : k + 1, :]
    last = [pltpu.make_async_copy(partial.at[my], parts.at[my], local.at[2])]
    for d in range(1, slab):
        last.append(pltpu.make_async_remote_copy(
            partial.at[lax.rem(my + d, slab)], parts.at[my], p_send.at[d], p_recv.at[d], **near(d)))
    run(last)
    out = next_shrink(variances, [effects[SWEEPS - 1, k] for k in range(slab)], weights, shrink)
    new_shrink[...] = out.reshape(width)
    wait(last)
    total = parts[0]
    for k in range(1, slab):
        total = total + parts[k]
    scores[...] = total / jnp.sqrt(live_total)


def per_device(samp, slab, ld_blocks, marginal, normals, block_len, scale_start, ancestry_weight, dosage):
    slots, size = ld_blocks.shape[1], ld_blocks.shape[2]
    width = slots * size
    rows = dosage.shape[0]
    quarter = width // slab
    vmem = pl.BlockSpec(memory_space=pltpu.VMEM)
    smem = pl.BlockSpec(memory_space=pltpu.SMEM)
    dma = pltpu.SemaphoreType.DMA
    effects, shrink, scores = pl.pallas_call(
        functools.partial(whole_kernel, samp, slab, slots, size),
        out_shape=(
            jax.ShapeDtypeStruct((1, width), F32),
            jax.ShapeDtypeStruct((width,), F32),
            jax.ShapeDtypeStruct((1, rows), F32),
        ),
        in_specs=[smem, smem] + [vmem] * 4 + [pl.BlockSpec(memory_space=pl.ANY)],
        out_specs=(vmem, vmem, vmem),
        scratch_shapes=[
            pltpu.VMEM((slots, size, size), F32),
            pltpu.VMEM((slots, TILE, TILE), F32),
            pltpu.VMEM((slots, TILE, TILE), F32),
            pltpu.VMEM((6 * TILE, size), BF16),
            pltpu.VMEM((slots, TILE, size), F32),
            pltpu.VMEM((SWEEPS, 1, width), F32),
            pltpu.VMEM((SWEEPS, 1, TILE), F32),
            pltpu.VMEM((SWEEPS, slab, 1, width), F32),
            pltpu.VMEM((SWEEPS, slab, 1, TILE), F32),
            pltpu.VMEM((SWEEPS, samp, slab, 1, TILE), F32),
            pltpu.VMEM((slab, 1, quarter), F32),
            pltpu.VMEM((samp, slab, 1, quarter), F32),
            pltpu.VMEM((16, dosage.shape[1]), BF16),
            pltpu.VMEM(dosage.shape, BF16),
            pltpu.VMEM((slab, 1, rows), F32),
            pltpu.VMEM((slab, 1, rows), F32),
            dma((SWEEPS, slab)), dma((SWEEPS, slab)), dma((SWEEPS, slab)), dma((SWEEPS, slab)),
            dma((SWEEPS, samp)), dma((SWEEPS, samp)), dma((slab,)), dma((slab,)), dma((samp,)), dma((samp,)),
            dma((slab,)), dma((slab,)), dma((4,)),
        ],
        compiler_params=pltpu.CompilerParams(collective_id=0, has_side_effects=True),
        name="sweeps",
    )(block_len, ancestry_weight, ld_blocks.reshape(slots, size, size), marginal, normals, scale_start, dosage)
    return (effects, shrink, scores.reshape(rows, 1))


def solution(mesh):
    return jax.shard_map(
        functools.partial(per_device, mesh.shape["samp"], mesh.shape["slab"]),
        mesh=mesh,
        in_specs=(
            P("slab", "samp", None, None),
            P("slab", "samp"),
            P(None, "slab", "samp"),
            P("samp"),
            P("samp"),
            P(),
            P("samp", "slab"),
        ),
        out_specs=(P("slab", "samp"), P("samp"), P("samp", "slab")),
        check_vma=False,
    )
```

```python
import functools

import jax
import jax.numpy as jnp
from jax import lax
from jax.experimental import pallas as pl
from jax.experimental.pallas import tpu as pltpu
from jax.sharding import PartitionSpec as P

SWEEPS = 2
TILE = 128
STEP = 8
GROUP = 64
SPREAD = 10
PIECES = 3
LEFT = (0, 0, 1, 1, 0, 2)
RIGHT = (0, 1, 0, 1, 2, 0)

shape_total = 1.5
global_shrink = 0.01

MESH = pl.DeviceIdType.MESH
F32 = jnp.float32
BF16 = jnp.bfloat16


def split3(x):
    high = x.astype(BF16)
    rest = x - high.astype(F32)
    mid = rest.astype(BF16)
    low = (rest - mid.astype(F32)).astype(BF16)
    return high, mid, low


def lane_spread(x, column):
    index = jnp.full(x.shape, column, jnp.int32)
    return jnp.take_along_axis(x, index, axis=1, mode="promise_in_bounds")


def row_spread(x, row):
    return jnp.broadcast_to(x[row : row + 1, :], x.shape)


def eliminate(slots, diag, fillers):
    lane = lax.broadcasted_iota(jnp.int32, (STEP, TILE), 1)
    sub = lax.broadcasted_iota(jnp.int32, (STEP, TILE), 0)
    steps = TILE // STEP
    emitted = 0
    for step in range(steps):
        first = step * STEP
        rows = pl.ds(first, STEP)
        value = [diag[b, rows, :] for b in range(slots)]
        columns = [[None] * STEP for _ in range(slots)]
        for j in range(STEP):
            for b in range(slots):
                columns[b][j] = lane_spread(value[b], first + j)
        held = list(value)
        pivots = list(value)
        for j in range(STEP):
            for b in range(slots):
                column = columns[b]
                pivot = row_spread(column[j], j)
                unit = jnp.where(sub == j, 1.0, 0.0)
                v = jnp.where(lane == first + j, unit, value[b])
                held[b] = jnp.where(sub == j, v, held[b])
                pivots[b] = jnp.where(sub == j, pivot, pivots[b])
                factor = jnp.where(sub == j, 0.0, column[j]) * (1.0 / pivot)
                value[b] = v - factor * row_spread(v, j)
                for k in range(j + 1, STEP):
                    column[k] = column[k] - factor * row_spread(column[k], j)
        later = range(step + 1, (first // GROUP + 1) * GROUP // STEP)
        solved = []
        for b in range(slots):
            root = lax.rsqrt(pivots[b])
            root = root * (1.5 - 0.5 * pivots[b] * root * root)
            diag[b, rows, :] = held[b] * root
            if later:
                whole = value[b] * (1.0 / pivots[b])
                solved.append([row_spread(whole, j) for j in range(STEP)])
        inside = (lane >= first) & (lane < first + STEP)
        below = {}
        total = {}
        for k in later:
            for b in range(slots):
                below[b, k] = diag[b, pl.ds(k * STEP, STEP), :]
                total[b, k] = jnp.where(inside, 0.0, below[b, k])
        for j in range(STEP):
            for k in later:
                for b in range(slots):
                    total[b, k] = total[b, k] - lane_spread(below[b, k], first + j) * solved[b][j]
        for k in later:
            for b in range(slots):
                diag[b, pl.ds(k * STEP, STEP), :] = total[b, k]
        due = min(len(fillers), -(-len(fillers) * (step + 1) // SPREAD))
        while emitted < due:
            fillers[emitted]()
            emitted += 1
        done = first + STEP
        if done % GROUP == 0 and done < TILE:
            group = pl.ds(done - GROUP, GROUP)
            wide = lax.broadcasted_iota(jnp.int32, (TILE - done, TILE), 1)
            gone = (wide >= done - GROUP) & (wide < done)
            group_lane = lax.broadcasted_iota(jnp.int32, (GROUP, TILE), 1)
            group_row = lax.broadcasted_iota(jnp.int32, (GROUP, TILE), 0) + (done - GROUP)
            upper = (group_lane > group_row) & (group_lane < done)
            for b in range(slots):
                pieces = split3(jnp.where(upper, 0.0, diag[b, group, :]))
                left = jnp.concatenate([pieces[i] for i in LEFT], axis=0).T
                right = jnp.concatenate([pieces[i] for i in RIGHT], axis=0)
                change = jnp.dot(left[done:, :], right, preferred_element_type=F32)
                rest = pl.ds(done, TILE - done)
                diag[b, rest, :] = jnp.where(gone, 0.0, diag[b, rest, :]) - change


def of_slot(value, b, size):
    return value[0:1, b * size : (b + 1) * size]


def solve(slots, size, length, ld, marginal, normals, shrink, noise_level,
          work, diag, terms, turned, inverses, forward, draws, residual, blend):
    tiles = size // TILE
    row = lax.broadcasted_iota(jnp.int32, (TILE, TILE), 0)
    col = lax.broadcasted_iota(jnp.int32, (TILE, TILE), 1)
    wide = lax.broadcasted_iota(jnp.int32, (1, size), 1)
    lives = [(wide < length[b]).astype(F32) for b in range(slots)]
    inverse = [lives[b] / of_slot(shrink, b, size) for b in range(slots)]

    def tile(p, count=1):
        return pl.ds(p * TILE, count * TILE)

    def loaded(b, r, c, count):
        across = lax.broadcasted_iota(jnp.int32, (TILE, count * TILE), 1) + c * TILE
        down = lax.broadcasted_iota(jnp.int32, (TILE, count * TILE), 0) + r * TILE
        inside = (down < length[b]) & (across < length[b])
        return jnp.where(inside, ld[b, tile(r), tile(c, count)].astype(F32), 0.0)

    def load_diagonal(b, r):
        at = slice(r * TILE, (r + 1) * TILE)
        extra = inverse[b][:, at] + (1.0 - lives[b][:, at])
        return loaded(b, r, r, 1) + jnp.where(row == col, extra, 0.0)

    def start_up(b):
        residual[b] = marginal[0:1, b * size : (b + 1) * size] * lives[b]
        blend[b] = jnp.zeros((1, size), F32)

    def load_rest(b, r):
        if r > 0:
            work[b, tile(r), tile(r)] = load_diagonal(b, r)
        if r + 1 < tiles:
            work[b, tile(r), tile(r + 1, tiles - r - 1)] = loaded(b, r, r + 1, tiles - r - 1)

    def draw_column(b, p):
        at = slice(p * TILE, (p + 1) * TILE)
        value = normals[0:1, pl.ds(b * size + p * TILE, TILE)] * lives[b][:, at]
        draws[b, p] = jnp.broadcast_to(value, (TILE, TILE)).T

    def make_rows(b, p, c, count):
        pieces = split3(inverses[b, p])
        left = jnp.concatenate([pieces[i] for i in LEFT], axis=1)
        pieces = split3(work[b, tile(p), tile(c, count)])
        right = jnp.concatenate([pieces[i] for i in RIGHT], axis=0)
        rows = jnp.dot(left, right, preferred_element_type=F32)
        work[b, tile(p), tile(c, count)] = rows
        for i, piece in enumerate(split3(rows)[:PIECES]):
            terms[b, p % 2, i, :, tile(c, count)] = piece

    def turn(b, p, k):
        for i in range(PIECES):
            turned[b, p % 2, tile(k), tile(i)] = terms[b, p % 2, i, :, tile(k)].T

    def product(b, p, k, rows, c, count):
        left = jnp.concatenate([turned[b, p % 2, tile(k, rows), tile(i)] for i in LEFT], axis=1)
        right = jnp.concatenate([terms[b, p % 2, i, :, tile(c, count)] for i in RIGHT], axis=0)
        return jnp.dot(left, right, preferred_element_type=F32)

    def trail(b, p, k, rows, c, count):
        work[b, tile(k, rows), tile(c, count)] = work[b, tile(k, rows), tile(c, count)] - product(b, p, k, rows, c, count)

    def step_forward(b, p):
        here = residual[b, :, tile(p)]
        column = jnp.sum(inverses[b, p] * here, axis=1, keepdims=True)
        column = jnp.broadcast_to(column, (TILE, TILE))
        forward[b, p] = column
        normal = draws[b, p]
        upper = jnp.where(col > row, work[b, tile(p), tile(p)], 0.0)
        pivot = jnp.where(col == row, 1.0 / jnp.where(col == row, inverses[b, p], 1.0), 0.0)
        blend[b, :, tile(p)] = blend[b, :, tile(p)] + jnp.sum((upper + pivot) * normal, axis=0, keepdims=True)
        for t in range(p + 1, tiles):
            rows = work[b, tile(p), tile(t)]
            residual[b, :, tile(t)] = residual[b, :, tile(t)] - jnp.sum(rows * column, axis=0, keepdims=True)
            blend[b, :, tile(t)] = blend[b, :, tile(t)] + jnp.sum(rows * normal, axis=0, keepdims=True)

    for b in range(slots):
        diag[b] = load_diagonal(b, 0)
    fillers = [functools.partial(start_up, b) for b in range(slots)]
    for r in range(tiles):
        for b in range(slots):
            fillers.append(functools.partial(load_rest, b, r))
            fillers.append(functools.partial(draw_column, b, r))
    for p in range(tiles):
        eliminate(slots, diag, fillers)
        fillers = []
        for b in range(slots):
            whole = diag[b]
            inverses[b, p] = jnp.where(col <= row, whole, 0.0)
            work[b, tile(p), tile(p)] = whole
        for b in range(slots):
            if p + 1 < tiles:
                make_rows(b, p, p + 1, 1)
                turn(b, p, p + 1)
                diag[b] = work[b, tile(p + 1), tile(p + 1)] - product(b, p, p + 1, 1, p + 1, 1)
        for b in range(slots):
            if p + 2 < tiles:
                fillers.append(functools.partial(make_rows, b, p, p + 2, tiles - p - 2))
        for b in range(slots):
            for k in range(p + 2, tiles):
                fillers.append(functools.partial(turn, b, p, k))
        for c in range(p + 2, tiles, 2):
            count = min(2, tiles - c)
            for b in range(slots):
                fillers.append(functools.partial(trail, b, p, p + 1, c + count - p - 1, c, count))
        for b in range(slots):
            fillers.append(functools.partial(step_forward, b, p))
    for filler in fillers:
        filler()

    solution_rows = [[None] * tiles for _ in range(slots)]
    for p in reversed(range(tiles)):
        for b in range(slots):
            weight = forward[b, p] + noise_level * draws[b, p]
            if p + 1 < tiles:
                known = jnp.zeros((TILE, TILE), F32)
                for t in range(p + 1, tiles):
                    known = known + work[b, tile(p), tile(t)] * solution_rows[b][t]
                weight = weight - jnp.sum(known, axis=1, keepdims=True)
            solution_rows[b][p] = jnp.sum(inverses[b, p] * weight, axis=0, keepdims=True)
    squares = jnp.zeros((1, size), F32)
    count = jnp.zeros((1, size), F32)
    drawn = []
    for b in range(slots):
        value = jnp.concatenate(solution_rows[b], axis=1) * lives[b]
        drawn.append(value)
        pull = inverse[b] * value
        misfit = pull - noise_level * blend[b] * lives[b]
        squares = squares + misfit * misfit + value * pull
        count = count + lives[b]
    lane = lax.broadcasted_iota(jnp.int32, (1, TILE), 1)
    stats = jnp.where(lane == 0, jnp.sum(squares), jnp.where(lane == 1, jnp.sum(count), 0.0))
    return jnp.concatenate(drawn, axis=1), stats


def variances_of(gathered, slab):
    total = jnp.sum(gathered[:, :, 0, :], axis=0)
    rows = [total[k : k + 1, :] for k in range(slab)]
    return [(r[0:1, 0:1] + 1.0) / (r[0:1, 1:2] + 1.0) for r in rows], rows[0][0:1, 1:2]


def next_shrink(variances, effects, weights, shrink):
    rate = shape_total / (shrink + global_shrink)
    pooled = jnp.zeros_like(shrink)
    for k, variance in enumerate(variances):
        effect = effects[k]
        pooled = pooled + weights[k] * effect * effect / variance
    return (pooled + 1.0) / (2.0 + jnp.sqrt(4.0 + 2.0 * rate * (pooled + 1.0)))


def whole_kernel(samp, slab, slots, size, length, weights_ref, ld, marginal, normals, scale, dosage,
                 mean, new_shrink, scores,
                 work, diag, terms, turned, inverses, forward, draws, residual, blend, state, level, drawn, stats, effects, own_stats, gathered,
                 quarters, columns, spread_columns, dose, partial, parts,
                 e_send, e_recv, s_send, s_recv, g_send, g_recv, q_send, q_recv, w_send, w_recv, p_send, p_recv, local):
    me, my = lax.axis_index("samp"), lax.axis_index("slab")
    width = slots * size
    quarter = width // slab
    barrier = pltpu.get_barrier_semaphore()

    def greet(d, carry):
        pl.semaphore_signal(barrier, inc=1, device_id=(lax.rem(me + d, samp), my), device_id_type=MESH)
        return carry

    lax.fori_loop(1, samp, greet, 0)
    for d in range(1, slab):
        pl.semaphore_signal(barrier, inc=1, device_id=(me, lax.rem(my + d, slab)), device_id_type=MESH)
    fetch = pltpu.make_async_copy(dosage, dose, local.at[0])
    fetch.start()
    weights = [weights_ref[k] for k in range(slab)]
    own_weight = weights[0]
    for k in range(1, slab):
        own_weight = jnp.where(my == k, weights[k], own_weight)

    def near(d):
        return dict(device_id=(me, lax.rem(my + d, slab)), device_id_type=MESH)

    def far(d):
        return dict(device_id=(lax.rem(me + d, samp), my), device_id_type=MESH)

    def run(copies):
        for copy in copies:
            copy.start()
        return copies

    def wait(copies):
        for copy in copies:
            copy.wait()

    state[...] = scale[...].reshape(1, width)
    level[...] = jnp.broadcast_to(jnp.sqrt(jnp.ones((1, 1), F32) / own_weight), (1, TILE))

    def near_copies(s):
        return [pltpu.make_async_remote_copy(
            stats.at[s], own_stats.at[s, my], s_send.at[s, d], s_recv.at[s, d], **near(d)) for d in range(1, slab)]

    def quarter_copies():
        copies = []
        for d in range(1, slab):
            theirs = pl.ds(pl.multiple_of(lax.rem(my + d, slab) * quarter, TILE), quarter)
            copies.append(pltpu.make_async_remote_copy(
                mean.at[:, theirs], quarters.at[my], q_send.at[d], q_recv.at[d], **near(d)))
        own = pl.ds(pl.multiple_of(my * quarter, TILE), quarter)
        return copies + [pltpu.make_async_copy(mean.at[:, own], quarters.at[my], local.at[3])]

    def effect_copies(s):
        copies = [pltpu.make_async_remote_copy(
            drawn.at[s], effects.at[s, my], e_send.at[s, d], e_recv.at[s, d], **near(d)) for d in range(1, slab)]
        return copies + [pltpu.make_async_copy(drawn.at[s], effects.at[s, my], local.at[2])]

    def stat_spread(s, d):
        return pltpu.make_async_remote_copy(
            own_stats.at[s], gathered.at[s, me], g_send.at[s, d], g_recv.at[s, d], **far(d))

    def column_spread(d):
        return pltpu.make_async_remote_copy(quarters, columns.at[me], w_send.at[d], w_recv.at[d], **far(d))

    def each(act):
        def one(d, carry):
            act(d)
            return carry

        lax.fori_loop(1, samp, one, 0)

    def sweep(s, carry):
        is_last = s == SWEEPS - 1
        shrink = state[...]
        effect, stat = solve(slots, size, length, ld, marginal, normals.at[s], shrink, level[0:1, 0:1],
                             work, diag, terms, turned, inverses, forward, draws, residual, blend)
        drawn[s] = effect
        stats[s] = stat

        @pl.when(s == 0)
        def _():
            mean[...] = effect
            pl.semaphore_wait(barrier, samp - 1 + slab - 1)

        @pl.when(s > 0)
        def _():
            mean[...] = mean[...] + effect

        @pl.when(is_last)
        def _():
            mean[...] = mean[...] / SWEEPS

        keep = pltpu.make_async_copy(stats.at[s], own_stats.at[s, my], local.at[1])
        run(near_copies(s) + [keep])

        @pl.when(is_last)
        def _():
            run(quarter_copies())

        run(effect_copies(s))
        wait(near_copies(s) + [keep])
        mine = pltpu.make_async_copy(own_stats.at[s], gathered.at[s, me], local.at[1])
        mine.start()
        each(lambda d: stat_spread(s, d).start())

        @pl.when(is_last)
        def _():
            wait(quarter_copies())
            pltpu.make_async_copy(quarters, columns.at[me], local.at[3]).start()
            each(lambda d: column_spread(d).start())

        wait(effect_copies(s))
        each(lambda d: stat_spread(s, d).wait())
        mine.wait()
        variances, _ = variances_of(gathered[s], slab)
        state[...] = next_shrink(variances, [effects[s, k] for k in range(slab)], weights, shrink)
        variance = variances[0]
        for k in range(1, slab):
            variance = jnp.where(my == k, variances[k], variance)
        level[...] = jnp.broadcast_to(jnp.sqrt(variance / own_weight), (1, TILE))
        return carry

    lax.fori_loop(0, SWEEPS, sweep, 0)
    new_shrink[...] = state[...].reshape(width)
    each(lambda d: column_spread(d).wait())
    pltpu.make_async_copy(quarters, columns.at[me], local.at[3]).wait()
    live_total = variances_of(gathered[SWEEPS - 1], slab)[1]
    fetch.wait()
    chunks = quarter // TILE

    def arrange(g, sums):
        for c in range(chunks):
            value = jnp.concatenate(
                [columns[g, k, :, pl.ds(c * TILE, TILE)] for k in range(slab)] + [jnp.zeros((16 - slab, TILE), F32)], axis=0)
            at = pl.ds(pl.multiple_of((g * chunks + c) * TILE, TILE), TILE)
            value = value.astype(BF16)
            spread_columns[:, at] = value
            sums = sums + value.astype(F32)
        return sums

    sums = lax.fori_loop(0, samp, arrange, jnp.zeros((16, TILE), F32))
    products = lax.dot_general(
        spread_columns[...], dose[...], (((1,), (1,)), ((), ())), preferred_element_type=F32)
    part = products - jnp.sum(sums, axis=1, keepdims=True)
    for k in range(slab):
        partial[k] = part[k : k + 1, :]
    last = [pltpu.make_async_copy(partial.at[my], parts.at[my], local.at[2])]
    for d in range(1, slab):
        last.append(pltpu.make_async_remote_copy(
            partial.at[lax.rem(my + d, slab)], parts.at[my], p_send.at[d], p_recv.at[d], **near(d)))
    run(last)
    wait(last)
    total = parts[0]
    for k in range(1, slab):
        total = total + parts[k]
    scores[...] = total / jnp.sqrt(live_total)


def per_device(samp, slab, ld_blocks, marginal, normals, block_len, scale_start, ancestry_weight, dosage):
    slots, size = ld_blocks.shape[1], ld_blocks.shape[2]
    width = slots * size
    rows = dosage.shape[0]
    quarter = width // slab
    vmem = pl.BlockSpec(memory_space=pltpu.VMEM)
    smem = pl.BlockSpec(memory_space=pltpu.SMEM)
    dma = pltpu.SemaphoreType.DMA
    effects, shrink, scores = pl.pallas_call(
        functools.partial(whole_kernel, samp, slab, slots, size),
        out_shape=(
            jax.ShapeDtypeStruct((1, width), F32),
            jax.ShapeDtypeStruct((width,), F32),
            jax.ShapeDtypeStruct((1, rows), F32),
        ),
        in_specs=[smem, smem] + [vmem] * 4 + [pl.BlockSpec(memory_space=pl.ANY)],
        out_specs=(vmem, vmem, vmem),
        scratch_shapes=[
            pltpu.VMEM((slots, size, size), F32),
            pltpu.VMEM((slots, TILE, TILE), F32),
            pltpu.VMEM((slots, 2, PIECES, TILE, size), BF16),
            pltpu.VMEM((slots, 2, size, PIECES * TILE), BF16),
            pltpu.VMEM((slots, size // TILE, TILE, TILE), F32),
            pltpu.VMEM((slots, size // TILE, TILE, TILE), F32),
            pltpu.VMEM((slots, size // TILE, TILE, TILE), F32),
            pltpu.VMEM((slots, 1, size), F32),
            pltpu.VMEM((slots, 1, size), F32),
            pltpu.VMEM((1, width), F32),
            pltpu.VMEM((1, TILE), F32),
            pltpu.VMEM((SWEEPS, 1, width), F32),
            pltpu.VMEM((SWEEPS, 1, TILE), F32),
            pltpu.VMEM((SWEEPS, slab, 1, width), F32),
            pltpu.VMEM((SWEEPS, slab, 1, TILE), F32),
            pltpu.VMEM((SWEEPS, samp, slab, 1, TILE), F32),
            pltpu.VMEM((slab, 1, quarter), F32),
            pltpu.VMEM((samp, slab, 1, quarter), F32),
            pltpu.VMEM((16, dosage.shape[1]), BF16),
            pltpu.VMEM(dosage.shape, BF16),
            pltpu.VMEM((slab, 1, rows), F32),
            pltpu.VMEM((slab, 1, rows), F32),
            dma((SWEEPS, slab)), dma((SWEEPS, slab)), dma((SWEEPS, slab)), dma((SWEEPS, slab)),
            dma((SWEEPS, samp)), dma((SWEEPS, samp)), dma((slab,)), dma((slab,)), dma((samp,)), dma((samp,)),
            dma((slab,)), dma((slab,)), dma((4,)),
        ],
        compiler_params=pltpu.CompilerParams(collective_id=0, has_side_effects=True),
        name="sweeps",
    )(block_len, ancestry_weight, ld_blocks.reshape(slots, size, size), marginal, normals, scale_start, dosage)
    return (effects, shrink, scores.reshape(rows, 1))


def solution(mesh):
    return jax.shard_map(
        functools.partial(per_device, mesh.shape["samp"], mesh.shape["slab"]),
        mesh=mesh,
        in_specs=(
            P("slab", "samp", None, None),
            P("slab", "samp"),
            P(None, "slab", "samp"),
            P("samp"),
            P("samp"),
            P(),
            P("samp", "slab"),
        ),
        out_specs=(P("slab", "samp"), P("samp"), P("samp", "slab")),
        check_vma=False,
    )
```

```python
import functools

import jax
import jax.numpy as jnp
from jax import lax
from jax.experimental import pallas as pl
from jax.experimental.pallas import tpu as pltpu
from jax.sharding import PartitionSpec as P

SWEEPS = 2
TILE = 128
STEP = 8
GROUP = 64
SPREAD = 10
PIECES = 3
LEFT = (0, 0, 1, 1, 0, 2)
RIGHT = (0, 1, 0, 1, 2, 0)

shape_total = 1.5
global_shrink = 0.01

MESH = pl.DeviceIdType.MESH
F32 = jnp.float32
BF16 = jnp.bfloat16


def split3(x):
    high = x.astype(BF16)
    rest = x - high.astype(F32)
    mid = rest.astype(BF16)
    low = (rest - mid.astype(F32)).astype(BF16)
    return high, mid, low


def lane_spread(x, column):
    index = jnp.full(x.shape, column, jnp.int32)
    return jnp.take_along_axis(x, index, axis=1, mode="promise_in_bounds")


def row_spread(x, row):
    return jnp.broadcast_to(x[row : row + 1, :], x.shape)


def eliminate(slots, diag, fillers):
    lane = lax.broadcasted_iota(jnp.int32, (STEP, TILE), 1)
    sub = lax.broadcasted_iota(jnp.int32, (STEP, TILE), 0)
    steps = TILE // STEP
    emitted = 0
    for step in range(steps):
        first = step * STEP
        rows = pl.ds(first, STEP)
        value = [diag[b, rows, :] for b in range(slots)]
        columns = [[None] * STEP for _ in range(slots)]
        for j in range(STEP):
            for b in range(slots):
                columns[b][j] = lane_spread(value[b], first + j)
        held = list(value)
        pivots = list(value)
        straight = list(value)
        crossed = list(value)
        for j in range(0, STEP, 2):
            pair = (sub == j) | (sub == j + 1)
            for b in range(slots):
                column = columns[b]
                left, right = column[j], column[j + 1]
                one = row_spread(left, j)
                two = row_spread(right, j + 1)
                mixed = row_spread(right, j)
                scale = 1.0 / (one * two - mixed * mixed)
                left = jnp.where(pair, 0.0, left)
                right = jnp.where(pair, 0.0, right)
                factor = (left * two - right * mixed) * scale
                second = (right * one - left * mixed) * scale
                for k in range(j + 2, STEP):
                    column[k] = (column[k] - factor * row_spread(column[k], j)) - second * row_spread(column[k], j + 1)
                slope = mixed * (1.0 / one)
                v = jnp.where(lane == first + j, jnp.where(sub == j, 1.0, 0.0), value[b])
                held[b] = jnp.where(sub == j, v, held[b])
                v = jnp.where(lane == first + j + 1, jnp.where(sub == j + 1, 1.0, 0.0), v)
                upper = row_spread(v, j)
                held[b] = jnp.where(sub == j + 1, v - slope * upper, held[b])
                pivots[b] = jnp.where(sub == j, one, jnp.where(sub == j + 1, two - mixed * slope, pivots[b]))
                straight[b] = jnp.where(sub == j, two * scale, jnp.where(sub == j + 1, one * scale, straight[b]))
                crossed[b] = jnp.where(pair, mixed * scale, crossed[b])
                value[b] = (v - factor * upper) - second * row_spread(v, j + 1)
        later = range(step + 1, (first // GROUP + 1) * GROUP // STEP)
        solved = []
        for b in range(slots):
            root = lax.rsqrt(pivots[b])
            root = root * (1.5 - 0.5 * pivots[b] * root * root)
            diag[b, rows, :] = held[b] * root
            if later:
                swapped = jnp.where(sub % 2 == 0, pltpu.roll(value[b], STEP - 1, 0), pltpu.roll(value[b], 1, 0))
                whole = value[b] * straight[b] - swapped * crossed[b]
                solved.append([row_spread(whole, j) for j in range(STEP)])
        inside = (lane >= first) & (lane < first + STEP)
        below = {}
        total = {}
        for k in later:
            for b in range(slots):
                below[b, k] = diag[b, pl.ds(k * STEP, STEP), :]
                total[b, k] = jnp.where(inside, 0.0, below[b, k])
        for k in later:
            for b in range(slots):
                parts = [lane_spread(below[b, k], first + j) * solved[b][j] for j in range(STEP)]
                while len(parts) > 1:
                    parts = [parts[i] + parts[i + 1] for i in range(0, len(parts), 2)]
                total[b, k] = total[b, k] - parts[0]
        for k in later:
            for b in range(slots):
                diag[b, pl.ds(k * STEP, STEP), :] = total[b, k]
        due = min(len(fillers), -(-len(fillers) * (step + 1) // SPREAD))
        while emitted < due:
            fillers[emitted]()
            emitted += 1
        done = first + STEP
        if done % GROUP == 0 and done < TILE:
            group = pl.ds(done - GROUP, GROUP)
            wide = lax.broadcasted_iota(jnp.int32, (TILE - done, TILE), 1)
            gone = (wide >= done - GROUP) & (wide < done)
            group_lane = lax.broadcasted_iota(jnp.int32, (GROUP, TILE), 1)
            group_row = lax.broadcasted_iota(jnp.int32, (GROUP, TILE), 0) + (done - GROUP)
            upper = (group_lane > group_row) & (group_lane < done)
            for b in range(slots):
                pieces = split3(jnp.where(upper, 0.0, diag[b, group, :]))
                left = jnp.concatenate([pieces[i] for i in LEFT], axis=0).T
                right = jnp.concatenate([pieces[i] for i in RIGHT], axis=0)
                change = jnp.dot(left[done:, :], right, preferred_element_type=F32)
                rest = pl.ds(done, TILE - done)
                diag[b, rest, :] = jnp.where(gone, 0.0, diag[b, rest, :]) - change


def of_slot(value, b, size):
    return value[0:1, b * size : (b + 1) * size]


def solve(slots, size, length, ld, marginal, normals, shrink, noise_level,
          work, diag, terms, turned, inverses, forward, draws, residual, blend):
    tiles = size // TILE
    row = lax.broadcasted_iota(jnp.int32, (TILE, TILE), 0)
    col = lax.broadcasted_iota(jnp.int32, (TILE, TILE), 1)
    wide = lax.broadcasted_iota(jnp.int32, (1, size), 1)
    lives = [(wide < length[b]).astype(F32) for b in range(slots)]
    inverse = [lives[b] / of_slot(shrink, b, size) for b in range(slots)]

    def tile(p, count=1):
        return pl.ds(p * TILE, count * TILE)

    def loaded(b, r, c, count):
        across = lax.broadcasted_iota(jnp.int32, (TILE, count * TILE), 1) + c * TILE
        down = lax.broadcasted_iota(jnp.int32, (TILE, count * TILE), 0) + r * TILE
        inside = (down < length[b]) & (across < length[b])
        return jnp.where(inside, ld[b, tile(r), tile(c, count)].astype(F32), 0.0)

    def load_diagonal(b, r):
        at = slice(r * TILE, (r + 1) * TILE)
        extra = inverse[b][:, at] + (1.0 - lives[b][:, at])
        return loaded(b, r, r, 1) + jnp.where(row == col, extra, 0.0)

    def start_up(b):
        residual[b] = marginal[0:1, b * size : (b + 1) * size] * lives[b]
        blend[b] = jnp.zeros((1, size), F32)

    def load_rest(b, r):
        if r > 0:
            work[b, tile(r), tile(r)] = load_diagonal(b, r)
        if r + 1 < tiles:
            work[b, tile(r), tile(r + 1, tiles - r - 1)] = loaded(b, r, r + 1, tiles - r - 1)

    def draw_column(b, p):
        at = slice(p * TILE, (p + 1) * TILE)
        value = normals[0:1, pl.ds(b * size + p * TILE, TILE)] * lives[b][:, at]
        draws[b, p] = jnp.broadcast_to(value, (TILE, TILE)).T

    def make_rows(b, p, c, count):
        pieces = split3(inverses[b, p])
        left = jnp.concatenate([pieces[i] for i in LEFT], axis=1)
        pieces = split3(work[b, tile(p), tile(c, count)])
        right = jnp.concatenate([pieces[i] for i in RIGHT], axis=0)
        rows = jnp.dot(left, right, preferred_element_type=F32)
        work[b, tile(p), tile(c, count)] = rows
        for i, piece in enumerate(split3(rows)[:PIECES]):
            terms[b, p % 2, i, :, tile(c, count)] = piece

    def turn(b, p, k):
        for i in range(PIECES):
            turned[b, p % 2, tile(k), tile(i)] = terms[b, p % 2, i, :, tile(k)].T

    def product(b, p, k, rows, c, count):
        left = jnp.concatenate([turned[b, p % 2, tile(k, rows), tile(i)] for i in LEFT], axis=1)
        right = jnp.concatenate([terms[b, p % 2, i, :, tile(c, count)] for i in RIGHT], axis=0)
        return jnp.dot(left, right, preferred_element_type=F32)

    def trail(b, p, k, rows, c, count):
        work[b, tile(k, rows), tile(c, count)] = work[b, tile(k, rows), tile(c, count)] - product(b, p, k, rows, c, count)

    def step_forward(b, p):
        here = residual[b, :, tile(p)]
        column = jnp.sum(inverses[b, p] * here, axis=1, keepdims=True)
        column = jnp.broadcast_to(column, (TILE, TILE))
        forward[b, p] = column
        normal = draws[b, p]
        upper = jnp.where(col > row, work[b, tile(p), tile(p)], 0.0)
        pivot = jnp.where(col == row, 1.0 / jnp.where(col == row, inverses[b, p], 1.0), 0.0)
        blend[b, :, tile(p)] = blend[b, :, tile(p)] + jnp.sum((upper + pivot) * normal, axis=0, keepdims=True)
        for t in range(p + 1, tiles):
            rows = work[b, tile(p), tile(t)]
            residual[b, :, tile(t)] = residual[b, :, tile(t)] - jnp.sum(rows * column, axis=0, keepdims=True)
            blend[b, :, tile(t)] = blend[b, :, tile(t)] + jnp.sum(rows * normal, axis=0, keepdims=True)

    for b in range(slots):
        diag[b] = load_diagonal(b, 0)
    fillers = [functools.partial(start_up, b) for b in range(slots)]
    for r in range(tiles):
        for b in range(slots):
            fillers.append(functools.partial(load_rest, b, r))
            fillers.append(functools.partial(draw_column, b, r))
    for p in range(tiles):
        eliminate(slots, diag, fillers)
        fillers = []
        for b in range(slots):
            whole = diag[b]
            inverses[b, p] = jnp.where(col <= row, whole, 0.0)
            work[b, tile(p), tile(p)] = whole
        for b in range(slots):
            if p + 1 < tiles:
                make_rows(b, p, p + 1, 1)
                turn(b, p, p + 1)
                diag[b] = work[b, tile(p + 1), tile(p + 1)] - product(b, p, p + 1, 1, p + 1, 1)
        for b in range(slots):
            if p + 2 < tiles:
                fillers.append(functools.partial(make_rows, b, p, p + 2, tiles - p - 2))
        for b in range(slots):
            for k in range(p + 2, tiles):
                fillers.append(functools.partial(turn, b, p, k))
        for c in range(p + 2, tiles, 2):
            count = min(2, tiles - c)
            for b in range(slots):
                fillers.append(functools.partial(trail, b, p, p + 1, c + count - p - 1, c, count))
        for b in range(slots):
            fillers.append(functools.partial(step_forward, b, p))
    for filler in fillers:
        filler()

    solution_rows = [[None] * tiles for _ in range(slots)]
    for p in reversed(range(tiles)):
        for b in range(slots):
            weight = forward[b, p] + noise_level * draws[b, p]
            if p + 1 < tiles:
                known = jnp.zeros((TILE, TILE), F32)
                for t in range(p + 1, tiles):
                    known = known + work[b, tile(p), tile(t)] * solution_rows[b][t]
                weight = weight - jnp.sum(known, axis=1, keepdims=True)
            solution_rows[b][p] = jnp.sum(inverses[b, p] * weight, axis=0, keepdims=True)
    squares = jnp.zeros((1, size), F32)
    count = jnp.zeros((1, size), F32)
    drawn = []
    for b in range(slots):
        value = jnp.concatenate(solution_rows[b], axis=1) * lives[b]
        drawn.append(value)
        pull = inverse[b] * value
        misfit = pull - noise_level * blend[b] * lives[b]
        squares = squares + misfit * misfit + value * pull
        count = count + lives[b]
    lane = lax.broadcasted_iota(jnp.int32, (1, TILE), 1)
    stats = jnp.where(lane == 0, jnp.sum(squares), jnp.where(lane == 1, jnp.sum(count), 0.0))
    return jnp.concatenate(drawn, axis=1), stats


def variances_of(gathered, slab):
    total = jnp.sum(gathered.reshape(-1, 8, TILE), axis=0)
    rows = []
    for k in range(slab):
        parts = [total[r : r + 1, :] for r in range(k, 8, slab)]
        rows.append(sum(parts[1:], parts[0]))
    return [(r[0:1, 0:1] + 1.0) / (r[0:1, 1:2] + 1.0) for r in rows], rows[0][0:1, 1:2]


def next_shrink(variances, effects, weights, shrink):
    rate = shape_total / (shrink + global_shrink)
    pooled = jnp.zeros_like(shrink)
    for k, variance in enumerate(variances):
        effect = effects[k]
        pooled = pooled + weights[k] * effect * effect / variance
    return (pooled + 1.0) / (2.0 + jnp.sqrt(4.0 + 2.0 * rate * (pooled + 1.0)))


def whole_kernel(samp, slab, slots, size, length, weights_ref, ld, marginal, normals, scale, dosage,
                 mean, new_shrink, scores,
                 work, diag, terms, turned, inverses, forward, draws, residual, blend, state, level, drawn, stats, effects, gathered, columns, spread_columns, dose, partial, parts,
                 e_send, e_recv, g_send, g_recv, w_send, w_recv, p_send, p_recv, local):
    me, my = lax.axis_index("samp"), lax.axis_index("slab")
    width = slots * size
    quarter = width // slab
    barrier = pltpu.get_barrier_semaphore()

    everyone = samp * slab
    own = me * slab + my

    def peer_of(d):
        peer = lax.rem(own + d, everyone)
        return lax.div(peer, slab), lax.rem(peer, slab)

    def far_first(d):
        return lax.rem(d + everyone // 2 - 2, everyone - 1) + 1

    def greet(d, carry):
        pl.semaphore_signal(barrier, inc=1, device_id=peer_of(d), device_id_type=MESH)
        return carry

    lax.fori_loop(1, everyone, greet, 0)
    fetch = pltpu.make_async_copy(dosage, dose, local.at[0])
    fetch.start()
    weights = [weights_ref[k] for k in range(slab)]
    own_weight = weights[0]
    for k in range(1, slab):
        own_weight = jnp.where(my == k, weights[k], own_weight)

    def near(d):
        return dict(device_id=(me, lax.rem(my + d, slab)), device_id_type=MESH)

    def run(copies):
        for copy in copies:
            copy.start()
        return copies

    def wait(copies):
        for copy in copies:
            copy.wait()

    state[...] = scale[...].reshape(1, width)
    level[...] = jnp.broadcast_to(jnp.sqrt(jnp.ones((1, 1), F32) / own_weight), (1, TILE))

    def effect_copies(s):
        copies = [pltpu.make_async_remote_copy(
            drawn.at[s], effects.at[s, my], e_send.at[s, d], e_recv.at[s, d], **near(d)) for d in range(1, slab)]
        return copies + [pltpu.make_async_copy(drawn.at[s], effects.at[s, my], local.at[2])]

    def stat_spread(s, d):
        return pltpu.make_async_remote_copy(
            stats.at[s], gathered.at[s, pl.ds(own, 1), :], g_send.at[s], g_recv.at[s],
            device_id=peer_of(d), device_id_type=MESH)

    def quarter_of(k):
        return mean.at[:, pl.ds(pl.multiple_of(k * quarter, TILE), quarter)]

    def column_spread(d):
        peer = peer_of(d)
        return pltpu.make_async_remote_copy(
            quarter_of(peer[1]), columns.at[me, my], w_send.at[0], w_recv.at[0],
            device_id=peer, device_id_type=MESH)

    def each(act):
        def one(d, carry):
            act(far_first(d))
            return carry

        lax.fori_loop(1, everyone, one, 0, unroll=4)

    def sweep(s, carry):
        is_last = s == SWEEPS - 1
        shrink = state[...]
        effect, stat = solve(slots, size, length, ld, marginal, normals.at[s], shrink, level[0:1, 0:1],
                             work, diag, terms, turned, inverses, forward, draws, residual, blend)
        drawn[s] = effect
        stats[s] = stat

        @pl.when(s == 0)
        def _():
            mean[...] = effect
            pl.semaphore_wait(barrier, everyone - 1)

        @pl.when(s > 0)
        def _():
            mean[...] = mean[...] + effect

        @pl.when(is_last)
        def _():
            mean[...] = mean[...] / SWEEPS

        each(lambda d: stat_spread(s, d).start())
        pltpu.make_async_copy(stats.at[s], gathered.at[s, pl.ds(own, 1), :], g_recv.at[s]).start()
        run(effect_copies(s))

        @pl.when(is_last)
        def _():
            each(lambda d: column_spread(d).start())
            pltpu.make_async_copy(quarter_of(my), columns.at[me, my], w_recv.at[0]).start()

        wait(effect_copies(s))
        pltpu.make_async_copy(gathered.at[s], gathered.at[s], g_recv.at[s]).wait()
        variances, _ = variances_of(gathered[s], slab)
        state[...] = next_shrink(variances, [effects[s, k] for k in range(slab)], weights, shrink)
        variance = variances[0]
        for k in range(1, slab):
            variance = jnp.where(my == k, variances[k], variance)
        level[...] = jnp.broadcast_to(jnp.sqrt(variance / own_weight), (1, TILE))
        return carry

    lax.fori_loop(0, SWEEPS, sweep, 0)
    new_shrink[...] = state[...].reshape(width)
    pltpu.make_async_copy(columns, columns, w_recv.at[0]).wait()
    live_total = variances_of(gathered[SWEEPS - 1], slab)[1]
    fetch.wait()
    chunks = quarter // TILE

    def arrange(g, sums):
        for c in range(chunks):
            value = jnp.concatenate(
                [columns[g, k, :, pl.ds(c * TILE, TILE)] for k in range(slab)] + [jnp.zeros((16 - slab, TILE), F32)], axis=0)
            at = pl.ds(pl.multiple_of((g * chunks + c) * TILE, TILE), TILE)
            value = value.astype(BF16)
            spread_columns[:, at] = value
            sums = sums + value.astype(F32)
        return sums

    sums = lax.fori_loop(0, samp, arrange, jnp.zeros((16, TILE), F32))
    products = lax.dot_general(
        spread_columns[...], dose[...], (((1,), (1,)), ((), ())), preferred_element_type=F32)
    part = products - jnp.sum(sums, axis=1, keepdims=True)
    for k in range(slab):
        partial[k] = part[k : k + 1, :]
    last = [pltpu.make_async_copy(partial.at[my], parts.at[my], local.at[2])]
    for d in range(1, slab):
        last.append(pltpu.make_async_remote_copy(
            partial.at[lax.rem(my + d, slab)], parts.at[my], p_send.at[d], p_recv.at[d], **near(d)))
    run(last)
    wait(last)
    for s in range(SWEEPS):
        sent = gathered.at[s, pl.ds(0, everyone - 1), :]
        pltpu.make_async_copy(sent, sent, g_send.at[s]).wait()

    def drain(d, carry):
        pltpu.make_async_copy(columns.at[0, 0], columns.at[0, 0], w_send.at[0]).wait()
        return carry

    lax.fori_loop(1, everyone, drain, 0)
    total = parts[0]
    for k in range(1, slab):
        total = total + parts[k]
    scores[...] = total / jnp.sqrt(live_total)


def hand_over(effects, shrink, scores, effects_out, shrink_out, scores_out):
    effects_out[...] = effects[...]
    shrink_out[...] = shrink[...]
    scores_out[...] = scores[...]


def per_device(samp, slab, ld_blocks, marginal, normals, block_len, scale_start, ancestry_weight, dosage):
    slots, size = ld_blocks.shape[1], ld_blocks.shape[2]
    width = slots * size
    rows = dosage.shape[0]
    quarter = width // slab
    vmem = pl.BlockSpec(memory_space=pltpu.VMEM)
    smem = pl.BlockSpec(memory_space=pltpu.SMEM)
    dma = pltpu.SemaphoreType.DMA
    effects, shrink, scores = pl.pallas_call(
        functools.partial(whole_kernel, samp, slab, slots, size),
        out_shape=(
            jax.ShapeDtypeStruct((1, width), F32),
            jax.ShapeDtypeStruct((width,), F32),
            jax.ShapeDtypeStruct((1, rows), F32),
        ),
        in_specs=[smem, smem] + [vmem] * 4 + [pl.BlockSpec(memory_space=pl.ANY)],
        out_specs=(vmem, vmem, vmem),
        scratch_shapes=[
            pltpu.VMEM((slots, size, size), F32),
            pltpu.VMEM((slots, TILE, TILE), F32),
            pltpu.VMEM((slots, 2, PIECES, TILE, size), BF16),
            pltpu.VMEM((slots, 2, size, PIECES * TILE), BF16),
            pltpu.VMEM((slots, size // TILE, TILE, TILE), F32),
            pltpu.VMEM((slots, size // TILE, TILE, TILE), F32),
            pltpu.VMEM((slots, size // TILE, TILE, TILE), F32),
            pltpu.VMEM((slots, 1, size), F32),
            pltpu.VMEM((slots, 1, size), F32),
            pltpu.VMEM((1, width), F32),
            pltpu.VMEM((1, TILE), F32),
            pltpu.VMEM((SWEEPS, 1, width), F32),
            pltpu.VMEM((SWEEPS, 1, TILE), F32),
            pltpu.VMEM((SWEEPS, slab, 1, width), F32),
            pltpu.VMEM((SWEEPS, samp * slab, TILE), F32),
            pltpu.VMEM((samp, slab, 1, quarter), F32),
            pltpu.VMEM((16, dosage.shape[1]), BF16),
            pltpu.VMEM(dosage.shape, BF16),
            pltpu.VMEM((slab, 1, rows), F32),
            pltpu.VMEM((slab, 1, rows), F32),
            dma((SWEEPS, slab)), dma((SWEEPS, slab)), dma((SWEEPS,)), dma((SWEEPS,)), dma((1,)), dma((1,)),
            dma((slab,)), dma((slab,)), dma((4,)),
        ],
        compiler_params=pltpu.CompilerParams(collective_id=0, has_side_effects=True),
        name="sweeps",
    )(block_len, ancestry_weight, ld_blocks.reshape(slots, size, size), marginal, normals, scale_start, dosage)
    effects, shrink, scores = pl.pallas_call(
        hand_over,
        out_shape=(
            jax.ShapeDtypeStruct((1, width), F32),
            jax.ShapeDtypeStruct((width,), F32),
            jax.ShapeDtypeStruct((1, rows), F32),
        ),
        in_specs=[vmem] * 3,
        out_specs=(vmem,) * 3,
        name="hand_over",
    )(effects, shrink, scores)
    return (effects, shrink, scores.reshape(rows, 1))


def solution(mesh):
    return jax.shard_map(
        functools.partial(per_device, mesh.shape["samp"], mesh.shape["slab"]),
        mesh=mesh,
        in_specs=(
            P("slab", "samp", None, None),
            P("slab", "samp"),
            P(None, "slab", "samp"),
            P("samp"),
            P("samp"),
            P(),
            P("samp", "slab"),
        ),
        out_specs=(P("slab", "samp"), P("samp"), P("samp", "slab")),
        check_vma=False,
    )
```

```python
import functools

import jax
import jax.numpy as jnp
from jax import lax
from jax.experimental import pallas as pl
from jax.experimental.pallas import tpu as pltpu
from jax.sharding import PartitionSpec as P

SWEEPS = 2
TILE = 128
STEP = 8
GROUP = 64
SPREAD = 10
PIECES = 3
LEFT = (0, 0, 1, 1, 0, 2)
RIGHT = (0, 1, 0, 1, 2, 0)

shape_total = 1.5
global_shrink = 0.01

MESH = pl.DeviceIdType.MESH
F32 = jnp.float32
BF16 = jnp.bfloat16


def split3(x):
    high = x.astype(BF16)
    rest = x - high.astype(F32)
    mid = rest.astype(BF16)
    low = (rest - mid.astype(F32)).astype(BF16)
    return high, mid, low


def lane_spread(x, column):
    index = jnp.full(x.shape, column, jnp.int32)
    return jnp.take_along_axis(x, index, axis=1, mode="promise_in_bounds")


def row_spread(x, row):
    return jnp.broadcast_to(x[row : row + 1, :], x.shape)


def eliminate(slots, diag, fillers):
    lane = lax.broadcasted_iota(jnp.int32, (STEP, TILE), 1)
    sub = lax.broadcasted_iota(jnp.int32, (STEP, TILE), 0)
    steps = TILE // STEP
    emitted = 0
    for step in range(steps):
        first = step * STEP
        rows = pl.ds(first, STEP)
        value = [diag[b, rows, :] for b in range(slots)]
        columns = [[None] * STEP for _ in range(slots)]
        for j in range(STEP):
            for b in range(slots):
                columns[b][j] = lane_spread(value[b], first + j)
        held = list(value)
        pivots = list(value)
        straight = list(value)
        crossed = list(value)
        for j in range(0, STEP, 2):
            pair = (sub == j) | (sub == j + 1)
            for b in range(slots):
                column = columns[b]
                left, right = column[j], column[j + 1]
                one = row_spread(left, j)
                two = row_spread(right, j + 1)
                mixed = row_spread(right, j)
                scale = 1.0 / (one * two - mixed * mixed)
                left = jnp.where(pair, 0.0, left)
                right = jnp.where(pair, 0.0, right)
                factor = (left * two - right * mixed) * scale
                second = (right * one - left * mixed) * scale
                for k in range(j + 2, STEP):
                    column[k] = (column[k] - factor * row_spread(column[k], j)) - second * row_spread(column[k], j + 1)
                slope = mixed * (1.0 / one)
                v = jnp.where(lane == first + j, jnp.where(sub == j, 1.0, 0.0), value[b])
                held[b] = jnp.where(sub == j, v, held[b])
                v = jnp.where(lane == first + j + 1, jnp.where(sub == j + 1, 1.0, 0.0), v)
                upper = row_spread(v, j)
                held[b] = jnp.where(sub == j + 1, v - slope * upper, held[b])
                pivots[b] = jnp.where(sub == j, one, jnp.where(sub == j + 1, two - mixed * slope, pivots[b]))
                straight[b] = jnp.where(sub == j, two * scale, jnp.where(sub == j + 1, one * scale, straight[b]))
                crossed[b] = jnp.where(pair, mixed * scale, crossed[b])
                value[b] = (v - factor * upper) - second * row_spread(v, j + 1)
        later = range(step + 1, (first // GROUP + 1) * GROUP // STEP)
        solved = []
        for b in range(slots):
            root = lax.rsqrt(pivots[b])
            root = root * (1.5 - 0.5 * pivots[b] * root * root)
            diag[b, rows, :] = held[b] * root
            if later:
                swapped = jnp.where(sub % 2 == 0, pltpu.roll(value[b], STEP - 1, 0), pltpu.roll(value[b], 1, 0))
                whole = value[b] * straight[b] - swapped * crossed[b]
                solved.append([row_spread(whole, j) for j in range(STEP)])
        inside = (lane >= first) & (lane < first + STEP)
        below = {}
        total = {}
        for k in later:
            for b in range(slots):
                below[b, k] = diag[b, pl.ds(k * STEP, STEP), :]
                total[b, k] = jnp.where(inside, 0.0, below[b, k])
        for k in later:
            for b in range(slots):
                parts = [lane_spread(below[b, k], first + j) * solved[b][j] for j in range(STEP)]
                while len(parts) > 1:
                    parts = [parts[i] + parts[i + 1] for i in range(0, len(parts), 2)]
                total[b, k] = total[b, k] - parts[0]
        for k in later:
            for b in range(slots):
                diag[b, pl.ds(k * STEP, STEP), :] = total[b, k]
        due = min(len(fillers), -(-len(fillers) * (step + 1) // SPREAD))
        while emitted < due:
            fillers[emitted]()
            emitted += 1
        done = first + STEP
        if done % GROUP == 0 and done < TILE:
            group = pl.ds(done - GROUP, GROUP)
            wide = lax.broadcasted_iota(jnp.int32, (TILE - done, TILE), 1)
            gone = (wide >= done - GROUP) & (wide < done)
            group_lane = lax.broadcasted_iota(jnp.int32, (GROUP, TILE), 1)
            group_row = lax.broadcasted_iota(jnp.int32, (GROUP, TILE), 0) + (done - GROUP)
            upper = (group_lane > group_row) & (group_lane < done)
            for b in range(slots):
                pieces = split3(jnp.where(upper, 0.0, diag[b, group, :]))
                left = jnp.concatenate([pieces[i] for i in LEFT], axis=0).T
                right = jnp.concatenate([pieces[i] for i in RIGHT], axis=0)
                change = jnp.dot(left[done:, :], right, preferred_element_type=F32)
                rest = pl.ds(done, TILE - done)
                diag[b, rest, :] = jnp.where(gone, 0.0, diag[b, rest, :]) - change


def of_slot(value, b, size):
    return value[0:1, b * size : (b + 1) * size]


def solve(slots, size, length, ld, marginal, normals, shrink, noise_level,
          work, diag, terms, turned, inverses, forward, draws, residual, blend):
    tiles = size // TILE
    row = lax.broadcasted_iota(jnp.int32, (TILE, TILE), 0)
    col = lax.broadcasted_iota(jnp.int32, (TILE, TILE), 1)
    wide = lax.broadcasted_iota(jnp.int32, (1, size), 1)
    lives = [(wide < length[b]).astype(F32) for b in range(slots)]
    inverse = [lives[b] / of_slot(shrink, b, size) for b in range(slots)]

    def tile(p, count=1):
        return pl.ds(p * TILE, count * TILE)

    def loaded(b, r, c, count):
        across = lax.broadcasted_iota(jnp.int32, (TILE, count * TILE), 1) + c * TILE
        down = lax.broadcasted_iota(jnp.int32, (TILE, count * TILE), 0) + r * TILE
        inside = (down < length[b]) & (across < length[b])
        return jnp.where(inside, ld[b, tile(r), tile(c, count)].astype(F32), 0.0)

    def load_diagonal(b, r):
        at = slice(r * TILE, (r + 1) * TILE)
        extra = inverse[b][:, at] + (1.0 - lives[b][:, at])
        return loaded(b, r, r, 1) + jnp.where(row == col, extra, 0.0)

    def start_up(b):
        residual[b] = marginal[0:1, b * size : (b + 1) * size] * lives[b]
        blend[b] = jnp.zeros((1, size), F32)

    def load_rest(b, r):
        if r > 0:
            work[b, tile(r), tile(r)] = load_diagonal(b, r)
        if r + 1 < tiles:
            work[b, tile(r), tile(r + 1, tiles - r - 1)] = loaded(b, r, r + 1, tiles - r - 1)

    def draw_column(b, p):
        at = slice(p * TILE, (p + 1) * TILE)
        value = normals[0:1, pl.ds(b * size + p * TILE, TILE)] * lives[b][:, at]
        draws[b, p] = jnp.broadcast_to(value, (TILE, TILE)).T

    def make_rows(b, p, c, count):
        pieces = split3(inverses[b, p])
        left = jnp.concatenate([pieces[i] for i in LEFT], axis=1)
        pieces = split3(work[b, tile(p), tile(c, count)])
        right = jnp.concatenate([pieces[i] for i in RIGHT], axis=0)
        rows = jnp.dot(left, right, preferred_element_type=F32)
        work[b, tile(p), tile(c, count)] = rows
        for i, piece in enumerate(split3(rows)[:PIECES]):
            terms[b, p % 2, i, :, tile(c, count)] = piece

    def turn(b, p, k):
        for i in range(PIECES):
            turned[b, p % 2, tile(k), tile(i)] = terms[b, p % 2, i, :, tile(k)].T

    def product(b, p, k, rows, c, count):
        left = jnp.concatenate([turned[b, p % 2, tile(k, rows), tile(i)] for i in LEFT], axis=1)
        right = jnp.concatenate([terms[b, p % 2, i, :, tile(c, count)] for i in RIGHT], axis=0)
        return jnp.dot(left, right, preferred_element_type=F32)

    def trail(b, p, k, rows, c, count):
        work[b, tile(k, rows), tile(c, count)] = work[b, tile(k, rows), tile(c, count)] - product(b, p, k, rows, c, count)

    def step_forward(b, p):
        here = residual[b, :, tile(p)]
        column = jnp.sum(inverses[b, p] * here, axis=1, keepdims=True)
        column = jnp.broadcast_to(column, (TILE, TILE))
        forward[b, p] = column
        normal = draws[b, p]
        upper = jnp.where(col > row, work[b, tile(p), tile(p)], 0.0)
        pivot = jnp.where(col == row, 1.0 / jnp.where(col == row, inverses[b, p], 1.0), 0.0)
        blend[b, :, tile(p)] = blend[b, :, tile(p)] + jnp.sum((upper + pivot) * normal, axis=0, keepdims=True)
        for t in range(p + 1, tiles):
            rows = work[b, tile(p), tile(t)]
            residual[b, :, tile(t)] = residual[b, :, tile(t)] - jnp.sum(rows * column, axis=0, keepdims=True)
            blend[b, :, tile(t)] = blend[b, :, tile(t)] + jnp.sum(rows * normal, axis=0, keepdims=True)

    for b in range(slots):
        diag[b] = load_diagonal(b, 0)
    fillers = [functools.partial(start_up, b) for b in range(slots)]
    for r in range(tiles):
        for b in range(slots):
            fillers.append(functools.partial(load_rest, b, r))
            fillers.append(functools.partial(draw_column, b, r))
    for p in range(tiles):
        eliminate(slots, diag, fillers)
        fillers = []
        for b in range(slots):
            whole = diag[b]
            inverses[b, p] = jnp.where(col <= row, whole, 0.0)
            work[b, tile(p), tile(p)] = whole
        for b in range(slots):
            if p + 1 < tiles:
                make_rows(b, p, p + 1, 1)
                turn(b, p, p + 1)
                diag[b] = work[b, tile(p + 1), tile(p + 1)] - product(b, p, p + 1, 1, p + 1, 1)
        for b in range(slots):
            if p + 2 < tiles:
                fillers.append(functools.partial(make_rows, b, p, p + 2, tiles - p - 2))
        for b in range(slots):
            for k in range(p + 2, tiles):
                fillers.append(functools.partial(turn, b, p, k))
        for c in range(p + 2, tiles, 2):
            count = min(2, tiles - c)
            for b in range(slots):
                fillers.append(functools.partial(trail, b, p, p + 1, c + count - p - 1, c, count))
        for b in range(slots):
            fillers.append(functools.partial(step_forward, b, p))
    for filler in fillers:
        filler()

    solution_rows = [[None] * tiles for _ in range(slots)]
    for p in reversed(range(tiles)):
        for b in range(slots):
            weight = forward[b, p] + noise_level * draws[b, p]
            if p + 1 < tiles:
                known = jnp.zeros((TILE, TILE), F32)
                for t in range(p + 1, tiles):
                    known = known + work[b, tile(p), tile(t)] * solution_rows[b][t]
                weight = weight - jnp.sum(known, axis=1, keepdims=True)
            solution_rows[b][p] = jnp.sum(inverses[b, p] * weight, axis=0, keepdims=True)
    drawn = [jnp.concatenate(solution_rows[b], axis=1) * lives[b] for b in range(slots)]

    def totals():
        squares = jnp.zeros((1, size), F32)
        count = jnp.zeros((1, size), F32)
        for b in range(slots):
            pull = inverse[b] * drawn[b]
            misfit = pull - noise_level * blend[b] * lives[b]
            squares = squares + misfit * misfit + drawn[b] * pull
            count = count + lives[b]
        lane = lax.broadcasted_iota(jnp.int32, (1, TILE), 1)
        return jnp.where(lane == 0, jnp.sum(squares), jnp.where(lane == 1, jnp.sum(count), 0.0))

    return jnp.concatenate(drawn, axis=1), totals


def variances_of(gathered, slab):
    total = jnp.sum(gathered.reshape(-1, 8, TILE), axis=0)
    rows = []
    for k in range(slab):
        parts = [total[r : r + 1, :] for r in range(k, 8, slab)]
        rows.append(sum(parts[1:], parts[0]))
    return [(r[0:1, 0:1] + 1.0) / (r[0:1, 1:2] + 1.0) for r in rows], rows[0][0:1, 1:2]


def next_shrink(variances, effects, weights, shrink):
    rate = shape_total / (shrink + global_shrink)
    pooled = jnp.zeros_like(shrink)
    for k, variance in enumerate(variances):
        effect = effects[k]
        pooled = pooled + weights[k] * effect * effect / variance
    return (pooled + 1.0) / (2.0 + jnp.sqrt(4.0 + 2.0 * rate * (pooled + 1.0)))


def whole_kernel(samp, slab, slots, size, length, weights_ref, ld, marginal, normals, scale, dosage,
                 mean, new_shrink, scores,
                 work, diag, terms, turned, inverses, forward, draws, residual, blend, state, level, drawn, stats, effects, gathered, columns, spread_columns, dose, partial, parts,
                 e_send, e_recv, g_send, g_recv, w_send, w_recv, p_send, p_recv, local):
    me, my = lax.axis_index("samp"), lax.axis_index("slab")
    width = slots * size
    quarter = width // slab
    barrier = pltpu.get_barrier_semaphore()

    everyone = samp * slab
    own = me * slab + my

    def peer_of(d):
        peer = lax.rem(own + d, everyone)
        return lax.div(peer, slab), lax.rem(peer, slab)

    def far_first(d):
        return lax.rem(d + everyone // 2 - 2, everyone - 1) + 1

    def greet(d, carry):
        pl.semaphore_signal(barrier, inc=1, device_id=peer_of(d), device_id_type=MESH)
        return carry

    lax.fori_loop(1, everyone, greet, 0)
    fetch = pltpu.make_async_copy(dosage, dose, local.at[0])
    fetch.start()
    weights = [weights_ref[k] for k in range(slab)]
    own_weight = weights[0]
    for k in range(1, slab):
        own_weight = jnp.where(my == k, weights[k], own_weight)

    def near(d):
        return dict(device_id=(me, lax.rem(my + d, slab)), device_id_type=MESH)

    def run(copies):
        for copy in copies:
            copy.start()
        return copies

    def wait(copies):
        for copy in copies:
            copy.wait()

    state[...] = scale[...].reshape(1, width)
    level[...] = jnp.broadcast_to(jnp.sqrt(jnp.ones((1, 1), F32) / own_weight), (1, TILE))

    def effect_copies(s):
        copies = [pltpu.make_async_remote_copy(
            drawn.at[s], effects.at[s, my], e_send.at[s, d], e_recv.at[s, d], **near(d)) for d in range(1, slab)]
        return copies + [pltpu.make_async_copy(drawn.at[s], effects.at[s, my], local.at[2])]

    def stat_spread(s, d):
        return pltpu.make_async_remote_copy(
            stats.at[s], gathered.at[s, pl.ds(own, 1), :], g_send.at[s], g_recv.at[s],
            device_id=peer_of(d), device_id_type=MESH)

    def quarter_of(k):
        return mean.at[:, pl.ds(pl.multiple_of(k * quarter, TILE), quarter)]

    def column_spread(d):
        peer = peer_of(d)
        return pltpu.make_async_remote_copy(
            quarter_of(peer[1]), columns.at[me, my], w_send.at[0], w_recv.at[0],
            device_id=peer, device_id_type=MESH)

    def each(act):
        def one(d, carry):
            act(far_first(d))
            return carry

        lax.fori_loop(1, everyone, one, 0, unroll=4)

    def sweep(s, carry):
        is_last = s == SWEEPS - 1
        shrink = state[...]
        effect, totals = solve(slots, size, length, ld, marginal, normals.at[s], shrink, level[0:1, 0:1],
                               work, diag, terms, turned, inverses, forward, draws, residual, blend)
        drawn[s] = effect

        @pl.when(s == 0)
        def _():
            mean[...] = effect
            pl.semaphore_wait(barrier, everyone - 1)

        @pl.when(s > 0)
        def _():
            mean[...] = mean[...] + effect

        @pl.when(is_last)
        def _():
            mean[...] = mean[...] / SWEEPS
            each(lambda d: column_spread(d).start())
            pltpu.make_async_copy(quarter_of(my), columns.at[me, my], w_recv.at[0]).start()

        run(effect_copies(s))
        stats[s] = totals()
        each(lambda d: stat_spread(s, d).start())
        pltpu.make_async_copy(stats.at[s], gathered.at[s, pl.ds(own, 1), :], g_recv.at[s]).start()

        @pl.when(s < SWEEPS - 1)
        def _():
            variances = update(s)
            variance = variances[0]
            for k in range(1, slab):
                variance = jnp.where(my == k, variances[k], variance)
            level[...] = jnp.broadcast_to(jnp.sqrt(variance / own_weight), (1, TILE))

        return carry

    def update(s):
        wait(effect_copies(s))
        pltpu.make_async_copy(gathered.at[s], gathered.at[s], g_recv.at[s]).wait()
        variances, _ = variances_of(gathered[s], slab)
        state[...] = next_shrink(variances, [effects[s, k] for k in range(slab)], weights, state[...])
        return variances

    lax.fori_loop(0, SWEEPS, sweep, 0)
    fetch.wait()
    chunks = quarter // TILE
    pltpu.make_async_copy(columns, columns, w_recv.at[0]).wait()

    def arrange(g, sums):
        for c in range(chunks):
            value = jnp.concatenate(
                [columns[g, k, :, pl.ds(c * TILE, TILE)] for k in range(slab)] + [jnp.zeros((16 - slab, TILE), F32)], axis=0)
            at = pl.ds(pl.multiple_of((g * chunks + c) * TILE, TILE), TILE)
            value = value.astype(BF16)
            spread_columns[:, at] = value
            sums = sums + value.astype(F32)
        return sums

    sums = lax.fori_loop(0, samp, arrange, jnp.zeros((16, TILE), F32), unroll=4)
    products = lax.dot_general(
        spread_columns[...], dose[...], (((1,), (1,)), ((), ())), preferred_element_type=F32)
    part = products - jnp.sum(sums, axis=1, keepdims=True)
    for k in range(slab):
        partial[k] = part[k : k + 1, :]
    last = [pltpu.make_async_copy(partial.at[my], parts.at[my], local.at[1])]
    for d in range(1, slab):
        last.append(pltpu.make_async_remote_copy(
            partial.at[lax.rem(my + d, slab)], parts.at[my], p_send.at[d], p_recv.at[d], **near(d)))
    run(last)
    update(SWEEPS - 1)
    new_shrink[...] = state[...].reshape(width)
    live_total = variances_of(gathered[SWEEPS - 1], slab)[1]
    for s in range(SWEEPS):
        sent = gathered.at[s, pl.ds(0, everyone - 1), :]
        pltpu.make_async_copy(sent, sent, g_send.at[s]).wait()

    def drain(d, carry):
        pltpu.make_async_copy(columns.at[0, 0], columns.at[0, 0], w_send.at[0]).wait()
        return carry

    lax.fori_loop(1, everyone, drain, 0)
    wait(last)
    total = parts[0]
    for k in range(1, slab):
        total = total + parts[k]
    scores[...] = total / jnp.sqrt(live_total)


def hand_over(effects, shrink, scores, effects_out, shrink_out, scores_out):
    effects_out[...] = effects[...]
    shrink_out[...] = shrink[...]
    scores_out[...] = scores[...]


def per_device(samp, slab, ld_blocks, marginal, normals, block_len, scale_start, ancestry_weight, dosage):
    slots, size = ld_blocks.shape[1], ld_blocks.shape[2]
    width = slots * size
    rows = dosage.shape[0]
    quarter = width // slab
    vmem = pl.BlockSpec(memory_space=pltpu.VMEM)
    smem = pl.BlockSpec(memory_space=pltpu.SMEM)
    dma = pltpu.SemaphoreType.DMA
    effects, shrink, scores = pl.pallas_call(
        functools.partial(whole_kernel, samp, slab, slots, size),
        out_shape=(
            jax.ShapeDtypeStruct((1, width), F32),
            jax.ShapeDtypeStruct((width,), F32),
            jax.ShapeDtypeStruct((1, rows), F32),
        ),
        in_specs=[smem, smem] + [vmem] * 4 + [pl.BlockSpec(memory_space=pl.ANY)],
        out_specs=(vmem, vmem, vmem),
        scratch_shapes=[
            pltpu.VMEM((slots, size, size), F32),
            pltpu.VMEM((slots, TILE, TILE), F32),
            pltpu.VMEM((slots, 2, PIECES, TILE, size), BF16),
            pltpu.VMEM((slots, 2, size, PIECES * TILE), BF16),
            pltpu.VMEM((slots, size // TILE, TILE, TILE), F32),
            pltpu.VMEM((slots, size // TILE, TILE, TILE), F32),
            pltpu.VMEM((slots, size // TILE, TILE, TILE), F32),
            pltpu.VMEM((slots, 1, size), F32),
            pltpu.VMEM((slots, 1, size), F32),
            pltpu.VMEM((1, width), F32),
            pltpu.VMEM((1, TILE), F32),
            pltpu.VMEM((SWEEPS, 1, width), F32),
            pltpu.VMEM((SWEEPS, 1, TILE), F32),
            pltpu.VMEM((SWEEPS, slab, 1, width), F32),
            pltpu.VMEM((SWEEPS, samp * slab, TILE), F32),
            pltpu.VMEM((samp, slab, 1, quarter), F32),
            pltpu.VMEM((16, dosage.shape[1]), BF16),
            pltpu.VMEM(dosage.shape, BF16),
            pltpu.VMEM((slab, 1, rows), F32),
            pltpu.VMEM((slab, 1, rows), F32),
            dma((SWEEPS, slab)), dma((SWEEPS, slab)), dma((SWEEPS,)), dma((SWEEPS,)), dma((1,)), dma((1,)),
            dma((slab,)), dma((slab,)), dma((4,)),
        ],
        compiler_params=pltpu.CompilerParams(collective_id=0, has_side_effects=True),
        name="sweeps",
    )(block_len, ancestry_weight, ld_blocks.reshape(slots, size, size), marginal, normals, scale_start, dosage)
    effects, shrink, scores = pl.pallas_call(
        hand_over,
        out_shape=(
            jax.ShapeDtypeStruct((1, width), F32),
            jax.ShapeDtypeStruct((width,), F32),
            jax.ShapeDtypeStruct((1, rows), F32),
        ),
        in_specs=[vmem] * 3,
        out_specs=(vmem,) * 3,
        name="hand_over",
    )(effects, shrink, scores)
    return (effects, shrink, scores.reshape(rows, 1))


def solution(mesh):
    return jax.shard_map(
        functools.partial(per_device, mesh.shape["samp"], mesh.shape["slab"]),
        mesh=mesh,
        in_specs=(
            P("slab", "samp", None, None),
            P("slab", "samp"),
            P(None, "slab", "samp"),
            P("samp"),
            P("samp"),
            P(),
            P("samp", "slab"),
        ),
        out_specs=(P("slab", "samp"), P("samp"), P("samp", "slab")),
        check_vma=False,
    )
```

```python
import functools

import jax
import jax.numpy as jnp
from jax import lax
from jax.experimental import pallas as pl
from jax.experimental.pallas import tpu as pltpu
from jax.sharding import PartitionSpec as P

SWEEPS = 2
TILE = 128
STEP = 8
GROUP = 64
SPREAD = 10
PIECES = 3
LEFT = (0, 0, 1, 1, 0, 2)
RIGHT = (0, 1, 0, 1, 2, 0)

shape_total = 1.5
global_shrink = 0.01

MESH = pl.DeviceIdType.MESH
F32 = jnp.float32
BF16 = jnp.bfloat16


def split3(x):
    high = x.astype(BF16)
    rest = x - high.astype(F32)
    mid = rest.astype(BF16)
    low = (rest - mid.astype(F32)).astype(BF16)
    return high, mid, low


def lane_spread(x, column):
    index = jnp.full(x.shape, column, jnp.int32)
    return jnp.take_along_axis(x, index, axis=1, mode="promise_in_bounds")


def row_spread(x, row):
    return jnp.broadcast_to(x[row : row + 1, :], x.shape)


def eliminate(slots, diag, fillers):
    lane = lax.broadcasted_iota(jnp.int32, (STEP, TILE), 1)
    sub = lax.broadcasted_iota(jnp.int32, (STEP, TILE), 0)
    steps = TILE // STEP
    emitted = 0
    for step in range(steps):
        first = step * STEP
        rows = pl.ds(first, STEP)
        value = [diag[b, rows, :] for b in range(slots)]
        columns = [[None] * STEP for _ in range(slots)]
        for j in range(STEP):
            for b in range(slots):
                columns[b][j] = lane_spread(value[b], first + j)
        held = list(value)
        pivots = list(value)
        straight = list(value)
        crossed = list(value)
        for j in range(0, STEP, 2):
            pair = (sub == j) | (sub == j + 1)
            for b in range(slots):
                column = columns[b]
                left, right = column[j], column[j + 1]
                one = row_spread(left, j)
                two = row_spread(right, j + 1)
                mixed = row_spread(right, j)
                scale = 1.0 / (one * two - mixed * mixed)
                left = jnp.where(pair, 0.0, left)
                right = jnp.where(pair, 0.0, right)
                factor = (left * two - right * mixed) * scale
                second = (right * one - left * mixed) * scale
                for k in range(j + 2, STEP):
                    column[k] = (column[k] - factor * row_spread(column[k], j)) - second * row_spread(column[k], j + 1)
                slope = mixed * (1.0 / one)
                v = jnp.where(lane == first + j, jnp.where(sub == j, 1.0, 0.0), value[b])
                held[b] = jnp.where(sub == j, v, held[b])
                v = jnp.where(lane == first + j + 1, jnp.where(sub == j + 1, 1.0, 0.0), v)
                upper = row_spread(v, j)
                held[b] = jnp.where(sub == j + 1, v - slope * upper, held[b])
                pivots[b] = jnp.where(sub == j, one, jnp.where(sub == j + 1, two - mixed * slope, pivots[b]))
                straight[b] = jnp.where(sub == j, two * scale, jnp.where(sub == j + 1, one * scale, straight[b]))
                crossed[b] = jnp.where(pair, mixed * scale, crossed[b])
                value[b] = (v - factor * upper) - second * row_spread(v, j + 1)
        later = range(step + 1, (first // GROUP + 1) * GROUP // STEP)
        solved = []
        for b in range(slots):
            root = lax.rsqrt(pivots[b])
            root = root * (1.5 - 0.5 * pivots[b] * root * root)
            diag[b, rows, :] = held[b] * root
            if later:
                swapped = jnp.where(sub % 2 == 0, pltpu.roll(value[b], STEP - 1, 0), pltpu.roll(value[b], 1, 0))
                whole = value[b] * straight[b] - swapped * crossed[b]
                solved.append([row_spread(whole, j) for j in range(STEP)])
        inside = (lane >= first) & (lane < first + STEP)
        below = {}
        total = {}
        for k in later:
            for b in range(slots):
                below[b, k] = diag[b, pl.ds(k * STEP, STEP), :]
                total[b, k] = jnp.where(inside, 0.0, below[b, k])
        for k in later:
            for b in range(slots):
                parts = [lane_spread(below[b, k], first + j) * solved[b][j] for j in range(STEP)]
                while len(parts) > 1:
                    parts = [parts[i] + parts[i + 1] for i in range(0, len(parts), 2)]
                total[b, k] = total[b, k] - parts[0]
        for k in later:
            for b in range(slots):
                diag[b, pl.ds(k * STEP, STEP), :] = total[b, k]
        due = min(len(fillers), -(-len(fillers) * (step + 1) // SPREAD))
        while emitted < due:
            fillers[emitted]()
            emitted += 1
        done = first + STEP
        if done % GROUP == 0 and done < TILE:
            group = pl.ds(done - GROUP, GROUP)
            wide = lax.broadcasted_iota(jnp.int32, (TILE - done, TILE), 1)
            gone = (wide >= done - GROUP) & (wide < done)
            group_lane = lax.broadcasted_iota(jnp.int32, (GROUP, TILE), 1)
            group_row = lax.broadcasted_iota(jnp.int32, (GROUP, TILE), 0) + (done - GROUP)
            upper = (group_lane > group_row) & (group_lane < done)
            for b in range(slots):
                pieces = split3(jnp.where(upper, 0.0, diag[b, group, :]))
                left = jnp.concatenate([pieces[i] for i in LEFT], axis=0).T
                right = jnp.concatenate([pieces[i] for i in RIGHT], axis=0)
                change = jnp.dot(left[done:, :], right, preferred_element_type=F32)
                rest = pl.ds(done, TILE - done)
                diag[b, rest, :] = jnp.where(gone, 0.0, diag[b, rest, :]) - change


def of_slot(value, b, size):
    return value[0:1, b * size : (b + 1) * size]


def solve(slots, size, length, ld, marginal, normals, shrink, noise_level,
          work, diag, terms, turned, inverses, forward, draws, residual, blend):
    tiles = size // TILE
    row = lax.broadcasted_iota(jnp.int32, (TILE, TILE), 0)
    col = lax.broadcasted_iota(jnp.int32, (TILE, TILE), 1)
    wide = lax.broadcasted_iota(jnp.int32, (1, size), 1)
    lives = [(wide < length[b]).astype(F32) for b in range(slots)]
    inverse = [lives[b] / of_slot(shrink, b, size) for b in range(slots)]

    def tile(p, count=1):
        return pl.ds(p * TILE, count * TILE)

    def loaded(b, r, c, count):
        across = lax.broadcasted_iota(jnp.int32, (TILE, count * TILE), 1) + c * TILE
        down = lax.broadcasted_iota(jnp.int32, (TILE, count * TILE), 0) + r * TILE
        inside = (down < length[b]) & (across < length[b])
        return jnp.where(inside, ld[b, tile(r), tile(c, count)].astype(F32), 0.0)

    def load_diagonal(b, r):
        at = slice(r * TILE, (r + 1) * TILE)
        extra = inverse[b][:, at] + (1.0 - lives[b][:, at])
        return loaded(b, r, r, 1) + jnp.where(row == col, extra, 0.0)

    def start_up(b):
        residual[b] = marginal[0:1, b * size : (b + 1) * size] * lives[b]
        blend[b] = jnp.zeros((1, size), F32)

    def load_rest(b, r):
        if r > 0:
            work[b, tile(r), tile(r)] = load_diagonal(b, r)
        if r + 1 < tiles:
            work[b, tile(r), tile(r + 1, tiles - r - 1)] = loaded(b, r, r + 1, tiles - r - 1)

    def draw_column(b, p):
        at = slice(p * TILE, (p + 1) * TILE)
        value = normals[0:1, pl.ds(b * size + p * TILE, TILE)] * lives[b][:, at]
        draws[b, p] = jnp.broadcast_to(value, (TILE, TILE)).T

    def make_rows(b, p, c, count):
        pieces = split3(inverses[b, p])
        left = jnp.concatenate([pieces[i] for i in LEFT], axis=1)
        pieces = split3(work[b, tile(p), tile(c, count)])
        right = jnp.concatenate([pieces[i] for i in RIGHT], axis=0)
        rows = jnp.dot(left, right, preferred_element_type=F32)
        work[b, tile(p), tile(c, count)] = rows
        for i, piece in enumerate(split3(rows)[:PIECES]):
            terms[b, p % 2, i, :, tile(c, count)] = piece

    def turn(b, p, k):
        for i in range(PIECES):
            turned[b, p % 2, tile(k), tile(i)] = terms[b, p % 2, i, :, tile(k)].T

    def product(b, p, k, rows, c, count):
        left = jnp.concatenate([turned[b, p % 2, tile(k, rows), tile(i)] for i in LEFT], axis=1)
        right = jnp.concatenate([terms[b, p % 2, i, :, tile(c, count)] for i in RIGHT], axis=0)
        return jnp.dot(left, right, preferred_element_type=F32)

    def trail(b, p, k, rows, c, count):
        work[b, tile(k, rows), tile(c, count)] = work[b, tile(k, rows), tile(c, count)] - product(b, p, k, rows, c, count)

    def step_forward(b, p):
        here = residual[b, :, tile(p)]
        column = jnp.sum(inverses[b, p] * here, axis=1, keepdims=True)
        column = jnp.broadcast_to(column, (TILE, TILE))
        forward[b, p] = column
        normal = draws[b, p]
        upper = jnp.where(col > row, work[b, tile(p), tile(p)], 0.0)
        pivot = jnp.where(col == row, 1.0 / jnp.where(col == row, inverses[b, p], 1.0), 0.0)
        blend[b, :, tile(p)] = blend[b, :, tile(p)] + jnp.sum((upper + pivot) * normal, axis=0, keepdims=True)
        for t in range(p + 1, tiles):
            rows = work[b, tile(p), tile(t)]
            residual[b, :, tile(t)] = residual[b, :, tile(t)] - jnp.sum(rows * column, axis=0, keepdims=True)
            blend[b, :, tile(t)] = blend[b, :, tile(t)] + jnp.sum(rows * normal, axis=0, keepdims=True)

    for b in range(slots):
        diag[b] = load_diagonal(b, 0)
    fillers = [functools.partial(start_up, b) for b in range(slots)]
    for r in range(tiles):
        for b in range(slots):
            fillers.append(functools.partial(load_rest, b, r))
            fillers.append(functools.partial(draw_column, b, r))
    for p in range(tiles):
        eliminate(slots, diag, fillers)
        fillers = []
        for b in range(slots):
            whole = diag[b]
            inverses[b, p] = jnp.where(col <= row, whole, 0.0)
            work[b, tile(p), tile(p)] = whole
        for b in range(slots):
            if p + 1 < tiles:
                make_rows(b, p, p + 1, 1)
                turn(b, p, p + 1)
                diag[b] = work[b, tile(p + 1), tile(p + 1)] - product(b, p, p + 1, 1, p + 1, 1)
        for b in range(slots):
            if p + 2 < tiles:
                fillers.append(functools.partial(make_rows, b, p, p + 2, tiles - p - 2))
        for b in range(slots):
            for k in range(p + 2, tiles):
                fillers.append(functools.partial(turn, b, p, k))
        for c in range(p + 2, tiles, 2):
            count = min(2, tiles - c)
            for b in range(slots):
                fillers.append(functools.partial(trail, b, p, p + 1, c + count - p - 1, c, count))
        for b in range(slots):
            fillers.append(functools.partial(step_forward, b, p))
    for filler in fillers:
        filler()

    solution_rows = [[None] * tiles for _ in range(slots)]
    for p in reversed(range(tiles)):
        for b in range(slots):
            weight = forward[b, p] + noise_level * draws[b, p]
            if p + 1 < tiles:
                known = jnp.zeros((TILE, TILE), F32)
                for t in range(p + 1, tiles):
                    known = known + work[b, tile(p), tile(t)] * solution_rows[b][t]
                weight = weight - jnp.sum(known, axis=1, keepdims=True)
            solution_rows[b][p] = jnp.sum(inverses[b, p] * weight, axis=0, keepdims=True)
    drawn = [jnp.concatenate(solution_rows[b], axis=1) * lives[b] for b in range(slots)]

    def totals():
        squares = jnp.zeros((1, size), F32)
        count = jnp.zeros((1, size), F32)
        for b in range(slots):
            pull = inverse[b] * drawn[b]
            misfit = pull - noise_level * blend[b] * lives[b]
            squares = squares + misfit * misfit + drawn[b] * pull
            count = count + lives[b]
        lane = lax.broadcasted_iota(jnp.int32, (1, TILE), 1)
        return jnp.where(lane == 0, jnp.sum(squares), jnp.where(lane == 1, jnp.sum(count), 0.0))

    return jnp.concatenate(drawn, axis=1), totals


def variances_of(gathered, slab):
    total = jnp.sum(gathered.reshape(-1, 8, TILE), axis=0)
    rows = []
    for k in range(slab):
        parts = [total[r : r + 1, :] for r in range(k, 8, slab)]
        rows.append(sum(parts[1:], parts[0]))
    return [(r[0:1, 0:1] + 1.0) / (r[0:1, 1:2] + 1.0) for r in rows], rows[0][0:1, 1:2]


def next_shrink(variances, effects, weights, shrink):
    rate = shape_total / (shrink + global_shrink)
    pooled = jnp.zeros_like(shrink)
    for k, variance in enumerate(variances):
        effect = effects[k]
        pooled = pooled + weights[k] * effect * effect / variance
    return (pooled + 1.0) / (2.0 + jnp.sqrt(4.0 + 2.0 * rate * (pooled + 1.0)))


def whole_kernel(samp, slab, slots, size, length, weights_ref, blocks, marginal, normals, scale, dosage,
                 mean, new_shrink, scores,
                 ld, work, diag, terms, turned, inverses, forward, draws, residual, blend, state, level, drawn, stats, effects, gathered, columns, spread_columns, dose, partial, parts,
                 e_send, e_recv, g_send, g_recv, w_send, w_recv, p_send, p_recv, local):
    me, my = lax.axis_index("samp"), lax.axis_index("slab")
    width = slots * size
    quarter = width // slab
    bring = pltpu.make_async_copy(blocks, ld, local.at[3])
    bring.start()
    fetch = pltpu.make_async_copy(dosage, dose, local.at[0])
    fetch.start()
    barrier = pltpu.get_barrier_semaphore()

    everyone = samp * slab
    own = me * slab + my

    def peer_of(d):
        peer = lax.rem(own + d, everyone)
        return lax.div(peer, slab), lax.rem(peer, slab)

    def far_first(d):
        return lax.rem(d + everyone // 2 - 2, everyone - 1) + 1

    def greet(d, carry):
        pl.semaphore_signal(barrier, inc=1, device_id=peer_of(d), device_id_type=MESH)
        return carry

    lax.fori_loop(1, everyone, greet, 0, unroll=4)
    weights = [weights_ref[k] for k in range(slab)]
    own_weight = weights[0]
    for k in range(1, slab):
        own_weight = jnp.where(my == k, weights[k], own_weight)

    def near(d):
        return dict(device_id=(me, lax.rem(my + d, slab)), device_id_type=MESH)

    def run(copies):
        for copy in copies:
            copy.start()
        return copies

    def wait(copies):
        for copy in copies:
            copy.wait()

    state[...] = scale[...].reshape(1, width)
    level[...] = jnp.broadcast_to(jnp.sqrt(jnp.ones((1, 1), F32) / own_weight), (1, TILE))

    def effect_copies(s):
        copies = [pltpu.make_async_remote_copy(
            drawn.at[s], effects.at[s, my], e_send.at[s, d], e_recv.at[s, d], **near(d)) for d in range(1, slab)]
        return copies + [pltpu.make_async_copy(drawn.at[s], effects.at[s, my], local.at[2])]

    def stat_spread(s, d):
        return pltpu.make_async_remote_copy(
            stats.at[s], gathered.at[s, pl.ds(own, 1), :], g_send.at[s], g_recv.at[s],
            device_id=peer_of(d), device_id_type=MESH)

    def quarter_of(k):
        return mean.at[:, pl.ds(pl.multiple_of(k * quarter, TILE), quarter)]

    def column_spread(d):
        peer = peer_of(d)
        return pltpu.make_async_remote_copy(
            quarter_of(peer[1]), columns.at[me, my], w_send.at[0], w_recv.at[0],
            device_id=peer, device_id_type=MESH)

    def each(act):
        def one(d, carry):
            act(far_first(d))
            return carry

        lax.fori_loop(1, everyone, one, 0, unroll=16)

    def sweep(s, carry):
        is_last = s == SWEEPS - 1
        shrink = state[...]
        effect, totals = solve(slots, size, length, ld, marginal, normals.at[s], shrink, level[0:1, 0:1],
                               work, diag, terms, turned, inverses, forward, draws, residual, blend)
        drawn[s] = effect

        @pl.when(s == 0)
        def _():
            mean[...] = effect
            pl.semaphore_wait(barrier, everyone - 1)

        @pl.when(s > 0)
        def _():
            mean[...] = mean[...] + effect

        @pl.when(is_last)
        def _():
            mean[...] = mean[...] / SWEEPS
            each(lambda d: column_spread(d).start())
            pltpu.make_async_copy(quarter_of(my), columns.at[me, my], w_recv.at[0]).start()

        run(effect_copies(s))
        stats[s] = totals()
        each(lambda d: stat_spread(s, d).start())
        pltpu.make_async_copy(stats.at[s], gathered.at[s, pl.ds(own, 1), :], g_recv.at[s]).start()

        @pl.when(s < SWEEPS - 1)
        def _():
            variances = update(s)
            variance = variances[0]
            for k in range(1, slab):
                variance = jnp.where(my == k, variances[k], variance)
            level[...] = jnp.broadcast_to(jnp.sqrt(variance / own_weight), (1, TILE))

        return carry

    def update(s):
        wait(effect_copies(s))
        pltpu.make_async_copy(gathered.at[s], gathered.at[s], g_recv.at[s]).wait()
        variances, _ = variances_of(gathered[s], slab)
        state[...] = next_shrink(variances, [effects[s, k] for k in range(slab)], weights, state[...])
        return variances

    bring.wait()
    lax.fori_loop(0, SWEEPS, sweep, 0)
    fetch.wait()
    chunks = quarter // TILE
    pltpu.make_async_copy(columns, columns, w_recv.at[0]).wait()

    def arrange(g, sums):
        for c in range(chunks):
            value = jnp.concatenate(
                [columns[g, k, :, pl.ds(c * TILE, TILE)] for k in range(slab)] + [jnp.zeros((16 - slab, TILE), F32)], axis=0)
            at = pl.ds(pl.multiple_of((g * chunks + c) * TILE, TILE), TILE)
            value = value.astype(BF16)
            spread_columns[:, at] = value
            sums = sums + value.astype(F32)
        return sums

    sums = lax.fori_loop(0, samp, arrange, jnp.zeros((16, TILE), F32), unroll=4)
    products = lax.dot_general(
        spread_columns[...], dose[...], (((1,), (1,)), ((), ())), preferred_element_type=F32)
    part = products - jnp.sum(sums, axis=1, keepdims=True)
    for k in range(slab):
        partial[k] = part[k : k + 1, :]
    last = [pltpu.make_async_copy(partial.at[my], parts.at[my], local.at[1])]
    for d in range(1, slab):
        last.append(pltpu.make_async_remote_copy(
            partial.at[lax.rem(my + d, slab)], parts.at[my], p_send.at[d], p_recv.at[d], **near(d)))
    run(last)
    update(SWEEPS - 1)
    new_shrink[...] = state[...].reshape(width)
    live_total = variances_of(gathered[SWEEPS - 1], slab)[1]
    for s in range(SWEEPS):
        sent = gathered.at[s, pl.ds(0, everyone - 1), :]
        pltpu.make_async_copy(sent, sent, g_send.at[s]).wait()

    def drain(d, carry):
        pltpu.make_async_copy(columns.at[0, 0], columns.at[0, 0], w_send.at[0]).wait()
        return carry

    lax.fori_loop(1, everyone, drain, 0)
    wait(last)
    total = parts[0]
    for k in range(1, slab):
        total = total + parts[k]
    scores[...] = total / jnp.sqrt(live_total)


def hand_over(effects, shrink, scores, effects_out, shrink_out, scores_out):
    effects_out[...] = effects[...]
    shrink_out[...] = shrink[...]
    scores_out[...] = scores[...]


def per_device(samp, slab, ld_blocks, marginal, normals, block_len, scale_start, ancestry_weight, dosage):
    slots, size = ld_blocks.shape[1], ld_blocks.shape[2]
    width = slots * size
    rows = dosage.shape[0]
    quarter = width // slab
    vmem = pl.BlockSpec(memory_space=pltpu.VMEM)
    smem = pl.BlockSpec(memory_space=pltpu.SMEM)
    dma = pltpu.SemaphoreType.DMA
    effects, shrink, scores = pl.pallas_call(
        functools.partial(whole_kernel, samp, slab, slots, size),
        out_shape=(
            jax.ShapeDtypeStruct((1, width), F32),
            jax.ShapeDtypeStruct((width,), F32),
            jax.ShapeDtypeStruct((1, rows), F32),
        ),
        in_specs=[smem, smem, pl.BlockSpec(memory_space=pl.ANY)] + [vmem] * 3 + [pl.BlockSpec(memory_space=pl.ANY)],
        out_specs=(vmem, vmem, vmem),
        scratch_shapes=[
            pltpu.VMEM((slots, size, size), BF16),
            pltpu.VMEM((slots, size, size), F32),
            pltpu.VMEM((slots, TILE, TILE), F32),
            pltpu.VMEM((slots, 2, PIECES, TILE, size), BF16),
            pltpu.VMEM((slots, 2, size, PIECES * TILE), BF16),
            pltpu.VMEM((slots, size // TILE, TILE, TILE), F32),
            pltpu.VMEM((slots, size // TILE, TILE, TILE), F32),
            pltpu.VMEM((slots, size // TILE, TILE, TILE), F32),
            pltpu.VMEM((slots, 1, size), F32),
            pltpu.VMEM((slots, 1, size), F32),
            pltpu.VMEM((1, width), F32),
            pltpu.VMEM((1, TILE), F32),
            pltpu.VMEM((SWEEPS, 1, width), F32),
            pltpu.VMEM((SWEEPS, 1, TILE), F32),
            pltpu.VMEM((SWEEPS, slab, 1, width), F32),
            pltpu.VMEM((SWEEPS, samp * slab, TILE), F32),
            pltpu.VMEM((samp, slab, 1, quarter), F32),
            pltpu.VMEM((16, dosage.shape[1]), BF16),
            pltpu.VMEM(dosage.shape, BF16),
            pltpu.VMEM((slab, 1, rows), F32),
            pltpu.VMEM((slab, 1, rows), F32),
            dma((SWEEPS, slab)), dma((SWEEPS, slab)), dma((SWEEPS,)), dma((SWEEPS,)), dma((1,)), dma((1,)),
            dma((slab,)), dma((slab,)), dma((4,)),
        ],
        compiler_params=pltpu.CompilerParams(collective_id=0, has_side_effects=True),
        name="sweeps",
    )(block_len, ancestry_weight, ld_blocks.reshape(slots, size, size), marginal, normals, scale_start, dosage)
    effects, shrink, scores = pl.pallas_call(
        hand_over,
        out_shape=(
            jax.ShapeDtypeStruct((1, width), F32),
            jax.ShapeDtypeStruct((width,), F32),
            jax.ShapeDtypeStruct((1, rows), F32),
        ),
        in_specs=[vmem] * 3,
        out_specs=(vmem,) * 3,
        name="hand_over",
    )(effects, shrink, scores)
    return (effects, shrink, scores.reshape(rows, 1))


def solution(mesh):
    return jax.shard_map(
        functools.partial(per_device, mesh.shape["samp"], mesh.shape["slab"]),
        mesh=mesh,
        in_specs=(
            P("slab", "samp", None, None),
            P("slab", "samp"),
            P(None, "slab", "samp"),
            P("samp"),
            P("samp"),
            P(),
            P("samp", "slab"),
        ),
        out_specs=(P("slab", "samp"), P("samp"), P("samp", "slab")),
        check_vma=False,
    )
```
